32 devices in a mesh: gx: 8 (over z, y), gy: 4 (over x, core).
Axes of the slice: x: 2, y: 2, z: 4, core: 2. Of those that a mesh axis runs over, the one named last changes fastest.
Arguments:
- state: float32 [4, 5, 5, 64, 1024], P(None, None, None, 'gy', 'gx'), may hold values from -3 to 60, as said below
Outputs:
- advanced: float32 [4, 5, 5, 64, 1024], P(None, None, None, 'gy', 'gx')
- tendency: float32 [4, 5, 5, 64, 1024], P(None, None, None, 'gy', 'gx')
The draws below stay inside these ranges and needn't reach their ends.
Inputs may be any that keep to these rules, and one draw needn't show every extreme that they name: `state`: at every node density is at least 0.2 and pressure, 0.4 times (energy minus half the squared momentum over density), is at least 0.2.
All inputs are finite; a program needn't handle non-finite values.
Results may differ from the reference program's by a relative error of at most 0.0003.
Values sent between devices are 32-bit elements; how exact they have to be, the bound alone decides.
A program may use at most 128 MiB of HBM per device.

```python
import math
import jax
import jax.numpy as jnp
import numpy as np
from jax import lax

NR = 64
NC = 1024


def draw_state(key, part):
    subkeys = jax.random.split(key, 6)
    column = jnp.arange(NC, dtype=jnp.float32)
    profile = 5.0 - 4.0 * jnp.cos(2.0 * math.pi * column / NC)
    shape_elem = (NR, NC)
    density = jax.random.uniform(subkeys[0], shape_elem, jnp.float32, 0.5, 1.5)
    pressure = profile * jax.random.uniform(subkeys[1], shape_elem, jnp.float32, 0.6, 1.4)
    jitter = jnp.clip(jax.random.normal(subkeys[2], (4, 5, 5, NR, NC), jnp.float32), -2.5, 2.5)
    drift_first = jax.random.uniform(subkeys[3], shape_elem, jnp.float32, -0.5, 0.5)
    drift_second = jax.random.uniform(subkeys[4], shape_elem, jnp.float32, -0.5, 0.5)
    amplitude = jnp.exp(jax.random.uniform(subkeys[5], shape_elem, jnp.float32, math.log(0.001), math.log(0.2)))
    node_density = density * (1.0 + amplitude * jitter[0])
    node_pressure = pressure * (1.0 + amplitude * jitter[3])
    node_first = drift_first + 0.5 * amplitude * jitter[1]
    node_second = drift_second + 0.5 * amplitude * jitter[2]
    energy = node_pressure / 0.4 + 0.5 * node_density * (node_first * node_first + node_second * node_second)
    return jnp.stack([node_density, node_density * node_first, node_density * node_second, energy]).astype(jnp.float32)


def setup_inputs(seed: int = 0) -> dict:
    streams_of = jax.random.split(jax.random.key(seed), 2)
    state = draw_state(jax.random.fold_in(streams_of[1], 71), 0)
    return {"state": state}


ADIABATIC = 1.4
COURANT = 0.2
ALPHA_MAX = 0.5

def tables():
    lobatto = np.array([-1.0, -math.sqrt(3.0 / 7.0), 0.0, math.sqrt(3.0 / 7.0), 1.0])
    weights = np.array([0.1, 49.0 / 90.0, 32.0 / 45.0, 49.0 / 90.0, 0.1])
    identity = np.eye(5)
    distance = lobatto[:, None] - lobatto[None, :] + identity
    barycentric = 1.0 / np.prod(distance, axis=1)
    derivative = (1.0 - identity) * (barycentric[None, :] / barycentric[:, None]) / distance
    derivative = derivative - identity * derivative.sum(axis=1)[:, None]
    legendre = np.zeros((5, 5))
    legendre[:, 0] = 1.0
    legendre[:, 1] = lobatto
    for degree in range(2, 5):
        legendre[:, degree] = ((2 * degree - 1) * lobatto * legendre[:, degree - 1] - (degree - 1) * legendre[:, degree - 2]) / degree
    norms = np.array([2.0, 2.0 / 3.0, 2.0 / 5.0, 2.0 / 7.0, 0.5])
    inverse = (legendre * weights[:, None]).T / norms[:, None]
    levels = np.maximum(np.arange(5)[:, None], np.arange(5)[None, :])
    return (jnp.asarray(derivative, jnp.float32), jnp.asarray(weights, jnp.float32), jnp.asarray(inverse, jnp.float32), jnp.asarray(levels == 4, jnp.float32), jnp.asarray(levels == 3, jnp.float32), jnp.asarray(levels <= 3, jnp.float32))

def slice_of(source, along_dim, begin_at, end_at):
    return lax.slice_in_dim(source, begin_at, end_at, axis=along_dim)

def slice_all(fields, along_dim, begin_at, end_at):
    return tuple((slice_of(member, along_dim, begin_at, end_at) for member in fields))

def primitive(conserved):
    density = conserved[0]
    speed_first = conserved[1] / density
    speed_second = conserved[2] / density
    pressure = (ADIABATIC - 1.0) * (conserved[3] - 0.5 * density * (speed_first * speed_first + speed_second * speed_second))
    return (density, speed_first, speed_second, pressure)

def log_mean(left_val, right_val):
    relative = (left_val * (left_val - 2.0 * right_val) + right_val * right_val) / (left_val * (left_val + 2.0 * right_val) + right_val * right_val)
    nearby = relative < 0.0001
    series = (left_val + right_val) * 52.5 / (105.0 + relative * (35.0 + relative * (21.0 + relative * 15.0)))
    logged = jnp.where(nearby, 1.0, jnp.log(right_val / left_val))
    return jnp.where(nearby, series, (right_val - left_val) / logged)

def two_point(left_state, right_state, normal_dir):
    mean_density = log_mean(left_state[0], right_state[0])
    thermal_mean = left_state[3] * right_state[3] / log_mean(left_state[0] * right_state[3], right_state[0] * left_state[3])
    mean_first = 0.5 * (left_state[1] + right_state[1])
    mean_second = 0.5 * (left_state[2] + right_state[2])
    mean_pressure = 0.5 * (left_state[3] + right_state[3])
    square_mean = 0.5 * (left_state[1] * right_state[1] + left_state[2] * right_state[2])
    left_normal = left_state[1 + normal_dir]
    right_normal = right_state[1 + normal_dir]
    mass_flux = mean_density * 0.5 * (left_normal + right_normal)
    push_first = mass_flux * mean_first + (mean_pressure if normal_dir == 0 else 0.0)
    push_second = mass_flux * mean_second + (mean_pressure if normal_dir == 1 else 0.0)
    energy_flux = mass_flux * (square_mean + thermal_mean / (ADIABATIC - 1.0)) + 0.5 * (left_state[3] * right_normal + right_state[3] * left_normal)
    return jnp.stack(jnp.broadcast_arrays(mass_flux, push_first, push_second, energy_flux))

def physical(primitives, normal_dir):
    normal_speed = primitives[1 + normal_dir]
    mass_flux = primitives[0] * normal_speed
    energy = primitives[3] / (ADIABATIC - 1.0) + 0.5 * primitives[0] * (primitives[1] * primitives[1] + primitives[2] * primitives[2])
    push_first = mass_flux * primitives[1] + (primitives[3] if normal_dir == 0 else 0.0)
    push_second = mass_flux * primitives[2] + (primitives[3] if normal_dir == 1 else 0.0)
    return jnp.stack([mass_flux, push_first, push_second, normal_speed * (energy + primitives[3])])

def wave(primitives, normal_dir):
    return jnp.abs(primitives[1 + normal_dir]) + jnp.sqrt(ADIABATIC * primitives[3] / primitives[0])

def direction_terms(conserved, primitives, normal_dir, derivative, weights):
    node_dim = 1 if normal_dir == 0 else 0
    elem_dim = 3 if normal_dir == 0 else 2
    flux_dim = node_dim + 1
    element_count = primitives[0].shape[elem_dim]
    shaper = [1, 1, 1, 1, 1]
    shaper[flux_dim] = 5
    volume = jnp.zeros(conserved.shape, jnp.float32)
    for partner in range(5):
        pair_flux = two_point(primitives, slice_all(primitives, node_dim, partner, partner + 1), normal_dir)
        volume = volume + (2.0 * derivative[:, partner]).reshape(tuple(shaper)) * pair_flux
    upper_trace = slice_all(primitives, node_dim, 4, 5)
    lower_trace = slice_all(primitives, node_dim, 0, 1)
    inner_left = slice_all(upper_trace, elem_dim, 0, element_count - 1)
    inner_right = slice_all(lower_trace, elem_dim, 1, element_count)
    state_left = slice_of(slice_of(conserved, flux_dim, 4, 5), elem_dim + 1, 0, element_count - 1)
    state_right = slice_of(slice_of(conserved, flux_dim, 0, 1), elem_dim + 1, 1, element_count)
    fastest = jnp.maximum(wave(inner_left, normal_dir), wave(inner_right, normal_dir))
    face_flux = two_point(inner_left, inner_right, normal_dir) - 0.5 * fastest * (state_right - state_left)
    flux_before = slice_of(face_flux, elem_dim + 1, 0, element_count - 2)
    flux_after = slice_of(face_flux, elem_dim + 1, 1, element_count - 1)
    inside = slice_all(primitives, elem_dim, 1, element_count - 1)
    inside_state = slice_of(conserved, elem_dim + 1, 1, element_count - 1)
    own_flux = physical(inside, normal_dir)
    volume = slice_of(volume, elem_dim + 1, 1, element_count - 1)
    middle = jnp.zeros_like(slice_of(own_flux, flux_dim, 0, 3))
    surface = jnp.concatenate([-(flux_before - slice_of(own_flux, flux_dim, 0, 1)) / weights[0], middle, (flux_after - slice_of(own_flux, flux_dim, 4, 5)) / weights[4]], axis=flux_dim)
    high_order = -(volume + surface)
    spread = jnp.maximum(wave(slice_all(inside, node_dim, 0, 4), normal_dir), wave(slice_all(inside, node_dim, 1, 5), normal_dir))
    subcell = 0.5 * (slice_of(own_flux, flux_dim, 0, 4) + slice_of(own_flux, flux_dim, 1, 5)) - 0.5 * spread * (slice_of(inside_state, flux_dim, 1, 5) - slice_of(inside_state, flux_dim, 0, 4))
    wall_flux = jnp.concatenate([flux_before, subcell, flux_after], axis=flux_dim)
    weight_column = weights.reshape(tuple(shaper))
    low_order = -(slice_of(wall_flux, flux_dim, 1, 6) - slice_of(wall_flux, flux_dim, 0, 5)) / weight_column
    return (high_order, low_order)

def blending(primitives, inverse, top_mask, next_mask, lower_mask):
    indicator = primitives[0] * primitives[3]
    modal_coef = jnp.einsum('ka,lb,abrc->klrc', inverse, inverse, indicator, precision=lax.Precision.HIGHEST)
    squares = modal_coef * modal_coef
    total_energy = lax.optimization_barrier(jnp.sum(squares, axis=(0, 1)))
    top_part = lax.optimization_barrier(jnp.sum(squares * top_mask[:, :, None, None], axis=(0, 1)))
    next_part = lax.optimization_barrier(jnp.sum(squares * next_mask[:, :, None, None], axis=(0, 1)))
    lower_part = lax.optimization_barrier(jnp.sum(squares * lower_mask[:, :, None, None], axis=(0, 1)))
    energy = jnp.maximum(top_part / total_energy, next_part / lower_part)
    threshold = 0.5 * 10.0 ** (-1.8 * 5.0 ** 0.25)
    sharpness = math.log((1.0 - 0.0001) / 0.0001)
    sigmoid_val = 1.0 / (1.0 + jnp.exp(-sharpness / threshold * (energy - threshold)))
    capped = jnp.minimum(sigmoid_val, ALPHA_MAX)
    centre = capped[1:-1, 1:-1]
    beside_all = jnp.maximum(jnp.maximum(capped[:-2, 1:-1], capped[2:, 1:-1]), jnp.maximum(capped[1:-1, :-2], capped[1:-1, 2:]))
    return jnp.maximum(centre, 0.5 * beside_all)

def tendency_of(conserved, table_set):
    derivative, weights, inverse, top_mask, next_mask, lower_mask = table_set
    primitives = primitive(conserved)
    high_columns, low_columns = direction_terms(conserved, primitives, 0, derivative, weights)
    high_rows, low_rows = direction_terms(conserved, primitives, 1, derivative, weights)
    blend_factor = blending(primitives, inverse, top_mask, next_mask, lower_mask)
    high_order = high_columns[:, :, :, 1:-1, :] + high_rows[:, :, :, :, 1:-1]
    low_order = low_columns[:, :, :, 1:-1, :] + low_rows[:, :, :, :, 1:-1]
    return (1.0 - blend_factor) * high_order + blend_factor * low_order

def full_tendency(conserved, table_set):
    padded = jnp.pad(conserved, ((0, 0), (0, 0), (0, 0), (1, 1), (1, 1)), mode='wrap')
    row_count = conserved.shape[3]
    block_rows = 16 if row_count % 16 == 0 else row_count

    def one_block(block_index):
        window = lax.dynamic_slice_in_dim(padded, block_index * block_rows, block_rows + 2, axis=3)
        return tendency_of(window, table_set)
    pieces = lax.map(one_block, jnp.arange(row_count // block_rows, dtype=jnp.int32))
    return jnp.moveaxis(pieces, 0, 3).reshape(conserved.shape)

def reference(state):
    table_set = tables()
    primitives = primitive(state)
    fastest = jnp.max(jnp.sqrt(primitives[1] * primitives[1] + primitives[2] * primitives[2]) + jnp.sqrt(ADIABATIC * primitives[3] / primitives[0]))
    delta_time = COURANT * 2.0 / (9.0 * fastest)
    rate_first = full_tendency(state, table_set)
    first_state = state + delta_time * rate_first
    rate_second = full_tendency(first_state, table_set)
    advanced = 0.5 * state + 0.5 * (first_state + delta_time * rate_second)
    return (advanced, rate_second)
```

```python
import functools
import math

import jax
import jax.numpy as jnp
import numpy as np
from jax import lax
from jax.experimental import pallas as pl
from jax.experimental.pallas import tpu as pltpu
from jax.sharding import PartitionSpec as P

MESH = pl.DeviceIdType.MESH
COURANT = 0.2
F32 = jnp.float32
LANES = 128
RHO, HX, HY, PR, LR, BE, LB, HC = range(8)


def tables():
    lobatto = np.array([-1.0, -math.sqrt(3.0 / 7.0), 0.0, math.sqrt(3.0 / 7.0), 1.0])
    weights = np.array([0.1, 49.0 / 90.0, 32.0 / 45.0, 49.0 / 90.0, 0.1])
    identity = np.eye(5)
    distance = lobatto[:, None] - lobatto[None, :] + identity
    barycentric = 1.0 / np.prod(distance, axis=1)
    derivative = (1.0 - identity) * (barycentric[None, :] / barycentric[:, None]) / distance
    legendre = np.zeros((5, 5))
    legendre[:, 0] = 1.0
    legendre[:, 1] = lobatto
    for degree in range(2, 5):
        legendre[:, degree] = (
            (2 * degree - 1) * lobatto * legendre[:, degree - 1]
            - (degree - 1) * legendre[:, degree - 2]
        ) / degree
    norms = np.array([2.0, 2.0 / 3.0, 2.0 / 5.0, 2.0 / 7.0, 0.5])
    inverse = (legendre * weights[:, None]).T / norms[:, None]
    return derivative, weights, inverse


DERIV, WEIGHTS, INVERSE = tables()
WINV = [float(1.0 / w) for w in WEIGHTS]


def coarse_inv(x):
    return pl.reciprocal(x, approx=True)


def inv(x):
    r = pl.reciprocal(x, approx=True)
    return r * (2.0 - x * r)


def series(f):
    return 2.0 + f * (2.0 / 3.0 + f * (2.0 / 5.0 + f * (2.0 / 7.0 + f * (2.0 / 9.0))))


def pair_flux(l, r, n):
    d = r[RHO] - l[RHO]
    s = r[RHO] + l[RHO]
    z = d * coarse_inv(s)
    f = z * z
    near = f < 0.03
    mean_rho = jnp.where(near, s, d) * inv(jnp.where(near, series(f), r[LR] - l[LR]))
    d2 = r[BE] - l[BE]
    s2 = r[BE] + l[BE]
    z2 = d2 * coarse_inv(s2)
    f2 = z2 * z2
    near2 = f2 < 0.03
    thermal = jnp.where(near2, series(f2), r[LB] - l[LB]) * inv(jnp.where(near2, s2, d2))
    hn, ht = (HX, HY) if n == 0 else (HY, HX)
    mass = mean_rho * (l[hn] + r[hn])
    normal = mass * (l[hn] + r[hn]) + 0.5 * (l[PR] + r[PR])
    tangent = mass * (l[ht] + r[ht])
    energy = mass * (2.0 * (l[HX] * r[HX] + l[HY] * r[HY]) + 2.5 * thermal) + (
        l[PR] * r[hn] + r[PR] * l[hn]
    )
    return (mass, normal, tangent, energy) if n == 0 else (mass, tangent, normal, energy)


def primitives_of(u):
    ri = inv(u[0])
    vx = u[1] * ri
    vy = u[2] * ri
    pressure = 0.4 * (u[3] - 0.5 * (u[1] * vx + u[2] * vy))
    beta = u[0] * inv(pressure)
    half_sound = jnp.sqrt(0.35 * pressure * ri)
    log_rho = jnp.log(u[0])
    log_beta = log_rho - jnp.log(pressure)
    return (u[0], 0.5 * vx, 0.5 * vy, pressure, log_rho, beta, log_beta, half_sound)


def face_of(l, r, el, er, n):
    flux = pair_flux(l, r, n)
    hn = HX if n == 0 else HY
    fast = jnp.maximum(jnp.abs(l[hn]) + l[HC], jnp.abs(r[hn]) + r[HC])
    fast2 = fast + fast
    return (
        flux[0] - fast * (r[RHO] - l[RHO]),
        flux[1] - fast2 * (r[RHO] * r[HX] - l[RHO] * l[HX]),
        flux[2] - fast2 * (r[RHO] * r[HY] - l[RHO] * l[HY]),
        flux[3] - fast * (er - el),
    )


def transform(values):
    v0, v1, v2, v3, v4 = values
    s0, s1, d0, d1 = v0 + v4, v1 + v3, v4 - v0, v3 - v1
    out = []
    for k in range(5):
        row = [float(c) for c in INVERSE[k]]
        if k % 2 == 0:
            out.append(row[0] * s0 + row[1] * s1 + row[2] * v2)
        else:
            out.append(row[4] * d0 + row[3] * d1)
    return out


def kernel(
    ngx, ngy, state, adv, tend,
    prim, first, rx, sx, fx, fy, raw, blend, packx, packy, gotx, goty,
    edge, top, top_got, top2, top2_got,
    hs, hr, ts, tr, t2s, t2r,
):
    gx = lax.axis_index("gx")
    gy = lax.axis_index("gy")
    at_x = lambda d: (lax.rem(gx + d, ngx), gy)
    at_y = lambda d: (gx, lax.rem(gy + d, ngy))
    rows = state.shape[2]
    halves = rows // 8

    barrier = pltpu.get_barrier_semaphore()
    for d in range(1, ngx):
        pl.semaphore_signal(barrier, inc=1, device_id=at_x(d), device_id_type=MESH)
    for d in range(1, ngy):
        pl.semaphore_signal(barrier, inc=1, device_id=at_y(d), device_id_type=MESH)

    lane = lax.broadcasted_iota(jnp.int32, (rows, LANES), 1)
    row = lax.broadcasted_iota(jnp.int32, (rows, LANES), 0)

    def tile(h):
        return pl.ds(pl.multiple_of(h * 8, 8), 8)

    def remote(src, dst, send, recv, device):
        return pltpu.make_async_remote_copy(
            src_ref=src, dst_ref=dst, send_sem=send, recv_sem=recv,
            device_id=device, device_id_type=MESH,
        )

    def halo_copies(sec):
        return [
            remote(packx.at[sec, 0], gotx.at[sec, 0], hs.at[sec, 0], hr.at[sec, 0], at_x(1)),
            remote(packx.at[sec, 1], gotx.at[sec, 1], hs.at[sec, 1], hr.at[sec, 1], at_x(ngx - 1)),
            remote(packy.at[sec, 0], goty.at[sec, 0], hs.at[sec, 2], hr.at[sec, 2], at_y(1)),
            remote(packy.at[sec, 1], goty.at[sec, 1], hs.at[sec, 3], hr.at[sec, 3], at_y(ngy - 1)),
        ]

    def indicator(sec):
        def body(h, carry):
            r = tile(h)
            lines = []
            for a in range(5):
                lines.append(
                    transform(
                        [prim[RHO, a * 5 + b, r, :] * prim[PR, a * 5 + b, r, :] for b in range(5)]
                    )
                )
            sums = {}
            for l in range(5):
                modes = transform([lines[a][l] for a in range(5)])
                for k in range(5):
                    level = max(k, l)
                    sq = modes[k] * modes[k]
                    key = level if level >= 3 else 0
                    sums[key] = sums[key] + sq if key in sums else sq
            lower = sums[0] + sums[3]
            total = lower + sums[4]
            level = jnp.maximum(sums[4] / total, sums[3] / lower)
            threshold = 0.5 * 10.0 ** (-1.8 * 5.0**0.25)
            sharp = math.log((1.0 - 0.0001) / 0.0001)
            value = 1.0 / (1.0 + jnp.exp((-sharp / threshold) * (level - threshold)))
            raw[r, :] = jnp.minimum(value, 0.5)
            return carry

        lax.fori_loop(0, halves, body, 0)

    def pack(sec, u):
        hi = jnp.where(lane == 5, pltpu.roll(raw[...], 6, 1), 0.0)
        lo = jnp.where(lane == 5, pltpu.roll(raw[...], 5, 1), 0.0)
        for v in range(4):
            for a in range(5):
                k = v * 8 + a
                hi = jnp.where(lane == k, pltpu.roll(u[v, a * 5 + 4], k + 1, 1), hi)
                low = u[v, a * 5]
                lo = jnp.where(lane == k, pltpu.roll(low, k, 1) if k else low, lo)
        packx[sec, 0] = hi
        packx[sec, 1] = lo
        packy[sec] = jnp.zeros(packy.shape[1:], F32)
        for v in range(4):
            for b in range(5):
                k = v * 8 + b
                packy[sec, 0, k : k + 1, :] = u[v, 20 + b, rows - 1 : rows, :]
                packy[sec, 1, k : k + 1, :] = u[v, b, 0:1, :]
        packy[sec, 0, 5:6, :] = raw[rows - 1 : rows, :]
        packy[sec, 1, 5:6, :] = raw[0:1, :]

    def faces(u):
        def body(i, carry):
            hi, lo = i * 5 + 4, i * 5
            l = [pltpu.roll(prim[q, hi], 1, 1) for q in range(8)]
            r = [prim[q, lo] for q in range(8)]
            flux = face_of(l, r, pltpu.roll(u[3, hi], 1, 1), u[3, lo], 0)
            for v in range(4):
                fx[i, 0, v] = flux[v]
                fx[i, 1, v] = pltpu.roll(flux[v], LANES - 1, 1)
            hi, lo = 20 + i, i
            l = [pltpu.roll(prim[q, hi], 1, 0) for q in range(8)]
            r = [prim[q, lo] for q in range(8)]
            flux = face_of(l, r, pltpu.roll(u[3, hi], 1, 0), u[3, lo], 1)
            for v in range(4):
                fy[i, 0, v] = flux[v]
                fy[i, 1, v] = pltpu.roll(flux[v], rows - 1, 0)
            return carry

        lax.fori_loop(0, 5, body, 0)

    def line_terms(n, node, r, u):
        def load(k):
            return [prim[q, node(k), r, :] for q in range(7)]

        acc = [[None] * 4 for _ in range(5)]
        for i in range(5):
            for j in range(i + 1, 5):
                q = float(2.0 * WEIGHTS[i] * DERIV[i, j])
                flux = pair_flux(load(i), load(j), n)
                for v in range(4):
                    term = q * flux[v]
                    acc[i][v] = term if acc[i][v] is None else acc[i][v] + term
                    acc[j][v] = -term if acc[j][v] is None else acc[j][v] - term
        hn = HX if n == 0 else HY

        def half(k):
            c = [u[v, node(k), r, :] for v in range(4)]
            speed = prim[hn, node(k), r, :]
            p = prim[PR, node(k), r, :]
            h = [0.5 * c[1 + n], speed * c[1], speed * c[2], speed * (c[3] + p)]
            h[1 + n] = h[1 + n] + 0.5 * p
            return c, h, jnp.abs(speed) + prim[HC, node(k), r, :]

        before = half(0)
        prev = None
        outs = []
        for k in range(5):
            if k < 4:
                after = half(k + 1)
                fast = jnp.maximum(before[2], after[2])
                g = [
                    before[1][v] + after[1][v] - fast * (after[0][v] - before[0][v])
                    for v in range(4)
                ]
                before = after
            for v in range(4):
                if k == 0:
                    t = g[v]
                elif k == 4:
                    t = -prev[v]
                else:
                    t = g[v] - prev[v]
                outs.append((k, v, acc[k][v] * -WINV[k], (acc[k][v] - t) * WINV[k]))
            prev = g
        return outs

    def volume_x(u):
        def body(i, carry):
            def inner(h, c):
                r = tile(h)
                for k, v, vol, diff in line_terms(0, lambda k: i * 5 + k, r, u):
                    rx[v, i * 5 + k, r, :] = vol
                    sx[v, i * 5 + k, r, :] = diff
                return c

            return lax.fori_loop(0, halves, inner, carry)

        lax.fori_loop(0, 5, body, 0)

    def finish_halo(sec):
        hi, lo = packx[sec, 0], packx[sec, 1]
        from_left, from_right = gotx[sec, 0], gotx[sec, 1]
        lslab = jnp.where(lane < 64, from_left, pltpu.roll(hi, 64, 1))
        rslab = jnp.where(lane < 64, lo, pltpu.roll(from_right, 64, 1))
        lu = [lslab if v == 0 else pltpu.roll(lslab, LANES - 8 * v, 1) for v in range(4)]
        ru = [rslab if v == 0 else pltpu.roll(rslab, LANES - 8 * v, 1) for v in range(4)]
        flux = face_of(primitives_of(lu), primitives_of(ru), lu[3], ru[3], 0)
        for a in range(5):
            for v in range(4):
                low = pltpu.roll(flux[v], LANES - a, 1) if a else flux[v]
                high = pltpu.roll(flux[v], 63 - a, 1)
                flo = jnp.where(lane == 0, low, fx[a, 0, v])
                fhi = jnp.where(lane == LANES - 1, high, fx[a, 1, v])
                rx[v, a * 5] = rx[v, a * 5] + WINV[0] * flo
                rx[v, a * 5 + 4] = rx[v, a * 5 + 4] - WINV[4] * fhi
        for side in range(2):
            lsrc = goty.at[sec, 0] if side == 0 else packy.at[sec, 0]
            rsrc = packy.at[sec, 1] if side == 0 else goty.at[sec, 1]
            lu = [lsrc[8 * v : 8 * v + 8, :] for v in range(4)]
            ru = [rsrc[8 * v : 8 * v + 8, :] for v in range(4)]
            flux = face_of(primitives_of(lu), primitives_of(ru), lu[3], ru[3], 1)
            for v in range(4):
                edge[side, v] = flux[v]
        for b in range(5):
            for v in range(4):
                fy[b, 0, v, 0:1, :] = edge[0, v, b : b + 1, :]
                fy[b, 1, v, rows - 1 : rows, :] = edge[1, v, b : b + 1, :]
        own = raw[...]
        left = jnp.where(lane == 0, pltpu.roll(from_left, LANES - 5, 1), pltpu.roll(own, 1, 1))
        right = jnp.where(
            lane == LANES - 1, pltpu.roll(from_right, LANES - 6, 1), pltpu.roll(own, LANES - 1, 1)
        )
        below = jnp.where(row == 0, goty[sec, 0, 5:6, :], pltpu.roll(own, 1, 0))
        above = jnp.where(row == rows - 1, goty[sec, 1, 5:6, :], pltpu.roll(own, rows - 1, 0))
        beside = jnp.maximum(jnp.maximum(left, right), jnp.maximum(below, above))
        blend[...] = jnp.maximum(own, 0.5 * beside)

    def volume_y(u, sink):
        def body(i, carry):
            def inner(h, c):
                r = tile(h)
                share = blend[r, :]
                for k, v, vol, diff in line_terms(1, lambda k: k * 5 + i, r, u):
                    m = k * 5 + i
                    rate = (rx[v, m, r, :] + vol) + share * (sx[v, m, r, :] + diff)
                    if k == 0:
                        rate = rate + WINV[0] * fy[i, 0, v, r, :]
                    if k == 4:
                        rate = rate - WINV[4] * fy[i, 1, v, r, :]
                    sink(v, m, r, rate)
                return c

            return lax.fori_loop(0, halves, inner, carry)

        lax.fori_loop(0, 5, body, 0)

    def prepare(m, fastest):
        q = primitives_of([state[v, m] for v in range(4)])
        for f in range(8):
            prim[f, m] = q[f]
        speed = jnp.sqrt(q[HX] * q[HX] + q[HY] * q[HY]) + q[HC]
        return jnp.maximum(fastest, speed)

    fastest = lax.fori_loop(0, 25, prepare, jnp.zeros((rows, LANES), F32))
    local_top = fastest[0:8]
    for h in range(1, halves):
        local_top = jnp.maximum(local_top, fastest[8 * h : 8 * h + 8])
    top[...] = local_top
    indicator(0)
    pack(0, state)
    pl.semaphore_wait(barrier, ngx + ngy - 2)
    halos = halo_copies(0)
    tops = [
        remote(top, top_got.at[d - 1], ts.at[d - 1], tr.at[d - 1], at_x(d)) for d in range(1, ngx)
    ]
    for copy in halos + tops:
        copy.start()
    faces(state)
    for copy in tops:
        copy.wait()
    local_top = top[...]
    for d in range(ngx - 1):
        local_top = jnp.maximum(local_top, top_got[d])
    top2[...] = local_top
    volume_x(state)
    tops = [
        remote(top2, top2_got.at[d - 1], t2s.at[d - 1], t2r.at[d - 1], at_y(d))
        for d in range(1, ngy)
    ]
    for copy in tops:
        copy.start()
    for copy in halos:
        copy.wait()
    finish_halo(0)

    def keep_rate(v, m, r, rate):
        tend[v, m, r, :] = rate

    volume_y(state, keep_rate)
    for copy in tops:
        copy.wait()
    local_top = top2[...]
    for d in range(ngy - 1):
        local_top = jnp.maximum(local_top, top2_got[d])
    step = (COURANT * 2.0 / 9.0) / (2.0 * jnp.max(local_top, keepdims=True))
    step = jnp.broadcast_to(step, (8, LANES))
    step_full = jnp.concatenate([step] * halves, axis=0)

    def prepare2(m, carry):
        u = [state[v, m] + step_full * tend[v, m] for v in range(4)]
        for v in range(4):
            first[v, m] = u[v]
        q = primitives_of(u)
        for f in range(8):
            prim[f, m] = q[f]
        return carry

    lax.fori_loop(0, 25, prepare2, 0)
    indicator(1)
    pack(1, first)
    faces(first)
    halos = halo_copies(1)
    for copy in halos:
        copy.start()
    volume_x(first)
    for copy in halos:
        copy.wait()
    finish_halo(1)

    def keep_both(v, m, r, rate):
        tend[v, m, r, :] = rate
        adv[v, m, r, :] = 0.5 * state[v, m, r, :] + 0.5 * (first[v, m, r, :] + step * rate)

    volume_y(first, keep_both)


def local(ngx, ngy, state):
    shape = state.shape
    rows, cols = shape[3], shape[4]
    flat = (4, 25, rows, cols)
    vmem = lambda *s: pltpu.VMEM(s, F32)
    out = pl.pallas_call(
        functools.partial(kernel, ngx, ngy),
        out_shape=(jax.ShapeDtypeStruct(flat, F32),) * 2,
        in_specs=[pl.BlockSpec(memory_space=pltpu.VMEM)],
        out_specs=[pl.BlockSpec(memory_space=pltpu.VMEM)] * 2,
        scratch_shapes=[
            vmem(8, 25, rows, cols),
            vmem(*flat), vmem(*flat), vmem(*flat),
            vmem(5, 2, 4, rows, cols), vmem(5, 2, 4, rows, cols),
            vmem(rows, cols), vmem(rows, cols),
            vmem(2, 2, rows, cols), vmem(2, 2, 32, cols),
            vmem(2, 2, rows, cols), vmem(2, 2, 32, cols),
            vmem(2, 4, 8, cols),
            vmem(8, cols), vmem(ngx - 1, 8, cols), vmem(8, cols), vmem(ngy - 1, 8, cols),
            pltpu.SemaphoreType.DMA((2, 4)), pltpu.SemaphoreType.DMA((2, 4)),
            pltpu.SemaphoreType.DMA((ngx - 1,)), pltpu.SemaphoreType.DMA((ngx - 1,)),
            pltpu.SemaphoreType.DMA((ngy - 1,)), pltpu.SemaphoreType.DMA((ngy - 1,)),
        ],
        compiler_params=pltpu.CompilerParams(collective_id=0, has_side_effects=True,
                                             vmem_limit_bytes=32 * 1024 * 1024),
        name="dg_two_sections",
    )(state.reshape(flat))
    return tuple(o.reshape(shape) for o in out)


def solution(mesh):
    spec = P(None, None, None, "gy", "gx")
    return jax.shard_map(
        functools.partial(local, mesh.shape["gx"], mesh.shape["gy"]),
        mesh=mesh,
        in_specs=(spec,),
        out_specs=(spec, spec),
        check_vma=False,
    )
```

```python
import functools
import math

import jax
import jax.numpy as jnp
import numpy as np
from jax import lax
from jax.experimental import pallas as pl
from jax.experimental.pallas import tpu as pltpu
from jax.sharding import PartitionSpec as P

MESH = pl.DeviceIdType.MESH
COURANT = 0.2
F32 = jnp.float32
LANES = 128
RHO, HX, HY, PR, LR, BE, LB, HC = range(8)
NEAR = 1.0 / 64.0
ENERGY = [1.0, 1.0, 1.0, 2.0]


def tables():
    lobatto = np.array([-1.0, -math.sqrt(3.0 / 7.0), 0.0, math.sqrt(3.0 / 7.0), 1.0])
    weights = np.array([0.1, 49.0 / 90.0, 32.0 / 45.0, 49.0 / 90.0, 0.1])
    identity = np.eye(5)
    distance = lobatto[:, None] - lobatto[None, :] + identity
    barycentric = 1.0 / np.prod(distance, axis=1)
    derivative = (1.0 - identity) * (barycentric[None, :] / barycentric[:, None]) / distance
    legendre = np.zeros((5, 5))
    legendre[:, 0] = 1.0
    legendre[:, 1] = lobatto
    for degree in range(2, 5):
        legendre[:, degree] = (
            (2 * degree - 1) * lobatto * legendre[:, degree - 1]
            - (degree - 1) * legendre[:, degree - 2]
        ) / degree
    norms = np.array([2.0, 2.0 / 3.0, 2.0 / 5.0, 2.0 / 7.0, 0.5])
    inverse = (legendre * weights[:, None]).T / norms[:, None]
    return derivative, weights, inverse


DERIV, WEIGHTS, INVERSE = tables()
WINV = [float(1.0 / w) for w in WEIGHTS]


def inv(x):
    return pl.reciprocal(x, approx=True)


def pair_flux(l, r, n, q=None):
    gap = r[LR] - l[LR]
    square = gap * gap
    even = (r[RHO] + l[RHO]) * (0.5 + square * (-1.0 / 24.0 + square * (1.0 / 240.0)))
    mean_rho = jnp.where(square < NEAR, even, (r[RHO] - l[RHO]) * inv(gap))
    gap2 = r[LB] - l[LB]
    square2 = gap2 * gap2
    near = square2 < NEAR * 1.25 * 1.25
    c1, c2 = 2.5 / 12.0 / 1.25**2, -2.5 / 720.0 / 1.25**4
    top = jnp.where(near, 2.5 + square2 * (c1 + square2 * c2), gap2)
    thermal = top * inv(jnp.where(near, r[BE] + l[BE], r[BE] - l[BE]))
    hn, ht = (HX, HY) if n == 0 else (HY, HX)
    along = l[hn] + r[hn]
    mass = mean_rho * along
    push = l[PR] + r[PR]
    work = l[PR] * r[hn] + r[PR] * l[hn]
    dot = l[HX] * r[HX] + l[HY] * r[HY]
    if q is not None:
        mass, push, work = q * mass, q * push, q * work
    normal = mass * along + push
    tangent = mass * (l[ht] + r[ht])
    energy = mass * (dot + thermal) + work
    return (mass, normal, tangent, energy) if n == 0 else (mass, tangent, normal, energy)


def primitives_of(u):
    ri = inv(u[0])
    vx = u[1] * ri
    vy = u[2] * ri
    pressure = 0.4 * (u[3] - 0.5 * (u[1] * vx + u[2] * vy))
    beta = u[0] * inv(pressure)
    half_sound = jnp.sqrt(0.35 * pressure * ri)
    log_rho = jnp.log(u[0])
    log_beta = 1.25 * (log_rho - jnp.log(pressure))
    return (u[0], 0.5 * vx, 0.5 * vy, 0.5 * pressure, log_rho, beta, log_beta, half_sound)


def face_of(l, r, el, er, n):
    flux = pair_flux(l, r, n)
    hn = HX if n == 0 else HY
    fast = jnp.maximum(jnp.abs(l[hn]) + l[HC], jnp.abs(r[hn]) + r[HC])
    fast2 = fast + fast
    return (
        flux[0] - fast * (r[RHO] - l[RHO]),
        flux[1] - fast2 * (r[RHO] * r[HX] - l[RHO] * l[HX]),
        flux[2] - fast2 * (r[RHO] * r[HY] - l[RHO] * l[HY]),
        flux[3] + flux[3] - fast * (er - el),
    )


def transform(values):
    v0, v1, v2, v3, v4 = values
    s0, s1, d0, d1 = v0 + v4, v1 + v3, v4 - v0, v3 - v1
    out = []
    for k in range(5):
        row = [float(c) for c in INVERSE[k]]
        if k % 2 == 0:
            out.append(row[0] * s0 + row[1] * s1 + row[2] * v2)
        else:
            out.append(row[4] * d0 + row[3] * d1)
    return out


def tile(h):
    return pl.ds(pl.multiple_of(h * 8, 8), 8)


def line_terms(prim, n, node, r, u):
    def load(k):
        return [prim[q, node(k), r, :] for q in range(7)]

    acc = [[None] * 4 for _ in range(5)]
    for i in range(5):
        for j in range(i + 1, 5):
            q = float(2.0 * WEIGHTS[i] * DERIV[i, j])
            flux = pair_flux(load(i), load(j), n, q)
            for v in range(4):
                term = flux[v]
                acc[i][v] = term if acc[i][v] is None else acc[i][v] + term
                acc[j][v] = -term if acc[j][v] is None else acc[j][v] - term
    hn = HX if n == 0 else HY

    def half(k):
        c = [u[v, node(k), r, :] for v in range(4)]
        speed = prim[hn, node(k), r, :]
        p = prim[PR, node(k), r, :]
        h = [0.5 * c[1 + n], speed * c[1], speed * c[2], speed * (0.5 * c[3] + p)]
        h[1 + n] = h[1 + n] + p
        return c, h, jnp.abs(speed) + prim[HC, node(k), r, :]

    before = half(0)
    prev = None
    outs = []
    for k in range(5):
        if k < 4:
            after = half(k + 1)
            fast = jnp.maximum(before[2], after[2])
            g = [
                before[1][v] + after[1][v]
                - (fast if v < 3 else 0.5 * fast) * (after[0][v] - before[0][v])
                for v in range(4)
            ]
            before = after
        for v in range(4):
            if k == 0:
                t = g[v]
            elif k == 4:
                t = -prev[v]
            else:
                t = g[v] - prev[v]
            w = WINV[k] * ENERGY[v]
            outs.append((k, v, acc[k][v] * -w, (acc[k][v] - t) * w))
        prev = g
    return outs


def column_y(i, prim, rx, sx, fy, blend, u, sink):
    def inner(h, c):
        r = tile(h)
        share = blend[r, :]
        for k, v, vol, diff in line_terms(prim, 1, lambda k: k * 5 + i, r, u):
            m = k * 5 + i
            rate = (rx[v, m, r, :] + vol) + share * (sx[v, m, r, :] + diff)
            if k == 0:
                rate = rate + WINV[0] * fy[i, 0, v, r, :]
            if k == 4:
                rate = rate - WINV[4] * fy[i, 1, v, r, :]
            sink(v, k, m, r, rate)
        return c

    lax.fori_loop(0, blend.shape[0] // 8, inner, 0)


def volume_y(prim, rx, sx, fy, blend, u, out):
    def body(i, carry):
        def sink(v, k, m, r, rate):
            out[v, m, r, :] = rate

        column_y(i, prim, rx, sx, fy, blend, u, sink)
        return carry

    lax.fori_loop(0, 5, body, 0)


def kernel(
    ngx, ngy, state_hbm, state, prim, first, rx, sx, fy, blend, step_ref,
    rate, fx, raw, packx, packy, gotx, goty,
    edge, top, top_got, top2, top2_got,
    ins, hs, hr, ts, tr, t2s, t2r,
):
    loads = [
        pltpu.make_async_copy(
            state_hbm.at[:, pl.ds(a * 5, 5)], state.at[:, pl.ds(a * 5, 5)], ins.at[a]
        )
        for a in range(5)
    ]
    for copy in loads:
        copy.start()
    gx = lax.axis_index("gx")
    gy = lax.axis_index("gy")
    at_x = lambda d: (lax.rem(gx + d, ngx), gy)
    at_y = lambda d: (gx, lax.rem(gy + d, ngy))
    rows = state.shape[2]
    halves = rows // 8

    barrier = pltpu.get_barrier_semaphore()
    for d in range(1, ngx):
        pl.semaphore_signal(barrier, inc=1, device_id=at_x(d), device_id_type=MESH)
    for d in range(1, ngy):
        pl.semaphore_signal(barrier, inc=1, device_id=at_y(d), device_id_type=MESH)

    lane = lax.broadcasted_iota(jnp.int32, (rows, LANES), 1)
    row = lax.broadcasted_iota(jnp.int32, (rows, LANES), 0)

    def remote(src, dst, send, recv, device):
        return pltpu.make_async_remote_copy(
            src_ref=src, dst_ref=dst, send_sem=send, recv_sem=recv,
            device_id=device, device_id_type=MESH,
        )

    def halo_copies(sec):
        return [
            remote(packx.at[sec, 0], gotx.at[sec, 0], hs.at[sec, 0], hr.at[sec, 0], at_x(1)),
            remote(packx.at[sec, 1], gotx.at[sec, 1], hs.at[sec, 1], hr.at[sec, 1], at_x(ngx - 1)),
            remote(packy.at[sec, 0], goty.at[sec, 0], hs.at[sec, 2], hr.at[sec, 2], at_y(1)),
            remote(packy.at[sec, 1], goty.at[sec, 1], hs.at[sec, 3], hr.at[sec, 3], at_y(ngy - 1)),
        ]

    def indicator(sec):
        def body(h, carry):
            r = tile(h)
            lines = []
            for a in range(5):
                lines.append(
                    transform(
                        [prim[RHO, a * 5 + b, r, :] * prim[PR, a * 5 + b, r, :] for b in range(5)]
                    )
                )
            sums = {}
            for l in range(5):
                modes = transform([lines[a][l] for a in range(5)])
                for k in range(5):
                    level = max(k, l)
                    sq = modes[k] * modes[k]
                    key = level if level >= 3 else 0
                    sums[key] = sums[key] + sq if key in sums else sq
            lower = sums[0] + sums[3]
            total = lower + sums[4]
            level = jnp.maximum(sums[4] / total, sums[3] / lower)
            threshold = 0.5 * 10.0 ** (-1.8 * 5.0**0.25)
            sharp = math.log((1.0 - 0.0001) / 0.0001)
            value = 1.0 / (1.0 + jnp.exp((-sharp / threshold) * (level - threshold)))
            raw[r, :] = jnp.minimum(value, 0.5)
            return carry

        lax.fori_loop(0, halves, body, 0)

    def pack(sec, u):
        hi = jnp.where(lane == 5, pltpu.roll(raw[...], 6, 1), 0.0)
        lo = jnp.where(lane == 5, pltpu.roll(raw[...], 5, 1), 0.0)
        for v in range(4):
            for a in range(5):
                k = v * 8 + a
                hi = jnp.where(lane == k, pltpu.roll(u[v, a * 5 + 4], k + 1, 1), hi)
                low = u[v, a * 5]
                lo = jnp.where(lane == k, pltpu.roll(low, k, 1) if k else low, lo)
        packx[sec, 0] = hi
        packx[sec, 1] = lo
        packy[sec] = jnp.zeros(packy.shape[1:], F32)
        for v in range(4):
            for b in range(5):
                k = v * 8 + b
                packy[sec, 0, k : k + 1, :] = u[v, 20 + b, rows - 1 : rows, :]
                packy[sec, 1, k : k + 1, :] = u[v, b, 0:1, :]
        packy[sec, 0, 5:6, :] = raw[rows - 1 : rows, :]
        packy[sec, 1, 5:6, :] = raw[0:1, :]

    def faces(u):
        def body(i, carry):
            hi, lo = i * 5 + 4, i * 5
            l = [pltpu.roll(prim[q, hi], 1, 1) for q in range(8)]
            r = [prim[q, lo] for q in range(8)]
            flux = face_of(l, r, pltpu.roll(u[3, hi], 1, 1), u[3, lo], 0)
            for v in range(4):
                fx[i, 0, v] = flux[v]
                fx[i, 1, v] = pltpu.roll(flux[v], LANES - 1, 1)
            hi, lo = 20 + i, i
            l = [pltpu.roll(prim[q, hi], 1, 0) for q in range(8)]
            r = [prim[q, lo] for q in range(8)]
            flux = face_of(l, r, pltpu.roll(u[3, hi], 1, 0), u[3, lo], 1)
            for v in range(4):
                fy[i, 0, v] = flux[v]
                fy[i, 1, v] = pltpu.roll(flux[v], rows - 1, 0)
            return carry

        lax.fori_loop(0, 5, body, 0)

    def volume_x(u):
        def body(i, carry):
            def inner(h, c):
                r = tile(h)
                for k, v, vol, diff in line_terms(prim, 0, lambda k: i * 5 + k, r, u):
                    rx[v, i * 5 + k, r, :] = vol
                    sx[v, i * 5 + k, r, :] = diff
                return c

            return lax.fori_loop(0, halves, inner, carry)

        lax.fori_loop(0, 5, body, 0)

    def finish_halo(sec):
        hi, lo = packx[sec, 0], packx[sec, 1]
        from_left, from_right = gotx[sec, 0], gotx[sec, 1]
        lslab = jnp.where(lane < 64, from_left, pltpu.roll(hi, 64, 1))
        rslab = jnp.where(lane < 64, lo, pltpu.roll(from_right, 64, 1))
        lu = [lslab if v == 0 else pltpu.roll(lslab, LANES - 8 * v, 1) for v in range(4)]
        ru = [rslab if v == 0 else pltpu.roll(rslab, LANES - 8 * v, 1) for v in range(4)]
        flux = face_of(primitives_of(lu), primitives_of(ru), lu[3], ru[3], 0)
        for a in range(5):
            for v in range(4):
                low = pltpu.roll(flux[v], LANES - a, 1) if a else flux[v]
                high = pltpu.roll(flux[v], 63 - a, 1)
                flo = jnp.where(lane == 0, low, fx[a, 0, v])
                fhi = jnp.where(lane == LANES - 1, high, fx[a, 1, v])
                rx[v, a * 5] = rx[v, a * 5] + WINV[0] * flo
                rx[v, a * 5 + 4] = rx[v, a * 5 + 4] - WINV[4] * fhi
        for side in range(2):
            lsrc = goty.at[sec, 0] if side == 0 else packy.at[sec, 0]
            rsrc = packy.at[sec, 1] if side == 0 else goty.at[sec, 1]
            lu = [lsrc[8 * v : 8 * v + 8, :] for v in range(4)]
            ru = [rsrc[8 * v : 8 * v + 8, :] for v in range(4)]
            flux = face_of(primitives_of(lu), primitives_of(ru), lu[3], ru[3], 1)
            for v in range(4):
                edge[side, v] = flux[v]
        for b in range(5):
            for v in range(4):
                fy[b, 0, v, 0:1, :] = edge[0, v, b : b + 1, :]
                fy[b, 1, v, rows - 1 : rows, :] = edge[1, v, b : b + 1, :]
        own = raw[...]
        left = jnp.where(lane == 0, pltpu.roll(from_left, LANES - 5, 1), pltpu.roll(own, 1, 1))
        right = jnp.where(
            lane == LANES - 1, pltpu.roll(from_right, LANES - 6, 1), pltpu.roll(own, LANES - 1, 1)
        )
        below = jnp.where(row == 0, goty[sec, 0, 5:6, :], pltpu.roll(own, 1, 0))
        above = jnp.where(row == rows - 1, goty[sec, 1, 5:6, :], pltpu.roll(own, rows - 1, 0))
        beside = jnp.maximum(jnp.maximum(left, right), jnp.maximum(below, above))
        blend[...] = jnp.maximum(own, 0.5 * beside)

    def prepare(a, fastest):
        for m in [a * 5 + b for b in range(5)]:
            q = primitives_of([state[v, m] for v in range(4)])
            for f in range(8):
                prim[f, m] = q[f]
            speed = jnp.sqrt(q[HX] * q[HX] + q[HY] * q[HY]) + q[HC]
            fastest = jnp.maximum(fastest, speed)
        return fastest

    def load_and_prepare(a, fastest):
        pltpu.make_async_copy(
            state_hbm.at[:, pl.ds(a * 5, 5)], state.at[:, pl.ds(a * 5, 5)], ins.at[a]
        ).wait()
        return prepare(a, fastest)

    fastest = lax.fori_loop(0, 5, load_and_prepare, jnp.zeros((rows, LANES), F32))
    local_top = fastest[0:8]
    for h in range(1, halves):
        local_top = jnp.maximum(local_top, fastest[8 * h : 8 * h + 8])
    top[...] = local_top
    indicator(0)
    pack(0, state)
    pl.semaphore_wait(barrier, ngx + ngy - 2)
    halos = halo_copies(0)
    tops = [
        remote(top, top_got.at[d - 1], ts.at[d - 1], tr.at[d - 1], at_x(d)) for d in range(1, ngx)
    ]
    for copy in halos + tops:
        copy.start()
    faces(state)
    volume_x(state)
    for copy in tops:
        copy.wait()
    local_top = top[...]
    for d in range(ngx - 1):
        local_top = jnp.maximum(local_top, top_got[d])
    top2[...] = local_top
    tops = [
        remote(top2, top2_got.at[d - 1], t2s.at[d - 1], t2r.at[d - 1], at_y(d))
        for d in range(1, ngy)
    ]
    for copy in tops:
        copy.start()
    for copy in halos:
        copy.wait()
    finish_halo(0)

    volume_y(prim, rx, sx, fy, blend, state, rate)
    for copy in tops:
        copy.wait()
    local_top = top2[...]
    for d in range(ngy - 1):
        local_top = jnp.maximum(local_top, top2_got[d])
    step = (COURANT * 2.0 / 9.0) / (2.0 * jnp.max(local_top, keepdims=True))
    step = jnp.broadcast_to(step, (8, LANES))
    step_full = jnp.concatenate([step] * halves, axis=0)

    def prepare2(a, carry):
        for m in [a * 5 + b for b in range(5)]:
            u = [state[v, m] + step_full * rate[v, m] for v in range(4)]
            for v in range(4):
                first[v, m] = u[v]
            q = primitives_of(u)
            for f in range(8):
                prim[f, m] = q[f]
        return carry

    lax.fori_loop(0, 5, prepare2, 0)
    indicator(1)
    pack(1, first)
    halos = halo_copies(1)
    for copy in halos:
        copy.start()
    step_ref[...] = step
    faces(first)
    volume_x(first)
    for copy in halos:
        copy.wait()
    finish_halo(1)


def last_kernel(state, prim, first, rx, sx, fy, blend, step_ref, adv, tend, adv_v, tend_v, sems):
    step = step_ref[...]

    def column(i):
        pairs = ((adv_v, adv), (tend_v, tend))
        return [
            pltpu.make_async_copy(src.at[i], dst.at[:, :, i], sems.at[k, i])
            for k, (src, dst) in enumerate(pairs)
        ]

    def body(i, carry):
        def sink(v, k, m, r, rate):
            tend_v[i, v, k, r, :] = rate
            adv_v[i, v, k, r, :] = 0.5 * state[v, m, r, :] + 0.5 * (
                first[v, m, r, :] + step * rate
            )

        column_y(i, prim, rx, sx, fy, blend, first, sink)
        for copy in column(i):
            copy.start()
        return carry

    lax.fori_loop(0, 5, body, 0)
    for i in range(5):
        for copy in column(i):
            copy.wait()


def local(ngx, ngy, state):
    shape = state.shape
    rows, cols = shape[3], shape[4]
    flat = (4, 25, rows, cols)
    vmem = lambda *s: pltpu.VMEM(s, F32)
    whole = pl.BlockSpec(memory_space=pltpu.VMEM)
    hbm = pl.BlockSpec(memory_space=pltpu.HBM)
    mid = [flat, (8, 25, rows, cols), flat, flat, flat, (5, 2, 4, rows, cols), (rows, cols), (8, cols)]
    kept = pl.pallas_call(
        functools.partial(kernel, ngx, ngy),
        out_shape=[jax.ShapeDtypeStruct(m, F32) for m in mid],
        in_specs=[hbm],
        out_specs=[whole] * len(mid),
        scratch_shapes=[
            vmem(*flat), vmem(5, 2, 4, rows, cols), vmem(rows, cols),
            vmem(2, 2, rows, cols), vmem(2, 2, 32, cols),
            vmem(2, 2, rows, cols), vmem(2, 2, 32, cols),
            vmem(2, 4, 8, cols),
            vmem(8, cols), vmem(ngx - 1, 8, cols), vmem(8, cols), vmem(ngy - 1, 8, cols),
            pltpu.SemaphoreType.DMA((5,)),
            pltpu.SemaphoreType.DMA((2, 4)), pltpu.SemaphoreType.DMA((2, 4)),
            pltpu.SemaphoreType.DMA((ngx - 1,)), pltpu.SemaphoreType.DMA((ngx - 1,)),
            pltpu.SemaphoreType.DMA((ngy - 1,)), pltpu.SemaphoreType.DMA((ngy - 1,)),
        ],
        compiler_params=pltpu.CompilerParams(collective_id=0, has_side_effects=True,
                                             vmem_limit_bytes=16 * 1024 * 1024),
        name="dg_sections",
    )(pltpu.with_memory_space_constraint(state.reshape(flat), pltpu.HBM))
    return pl.pallas_call(
        last_kernel,
        out_shape=(jax.ShapeDtypeStruct(shape, F32),) * 2,
        in_specs=[whole] * len(mid),
        out_specs=[hbm] * 2,
        scratch_shapes=[
            vmem(5, 4, 5, rows, cols), vmem(5, 4, 5, rows, cols), pltpu.SemaphoreType.DMA((2, 5))
        ],
        compiler_params=pltpu.CompilerParams(vmem_limit_bytes=16 * 1024 * 1024),
        name="dg_last_pass",
    )(*kept)


def solution(mesh):
    spec = P(None, None, None, "gy", "gx")
    return jax.shard_map(
        functools.partial(local, mesh.shape["gx"], mesh.shape["gy"]),
        mesh=mesh,
        in_specs=(spec,),
        out_specs=(spec, spec),
        check_vma=False,
    )
```

```python
import functools
import math

import jax
import jax.numpy as jnp
import numpy as np
from jax import lax
from jax.experimental import pallas as pl
from jax.experimental.pallas import tpu as pltpu
from jax.sharding import PartitionSpec as P

MESH = pl.DeviceIdType.MESH
COURANT = 0.2
F32 = jnp.float32
LANES = 128
RHO, HX, HY, PR, LR, BE, LB, HC = range(8)
NEAR = 1.0 / 64.0
EARLY = 2
ENERGY = [1.0, 1.0, 1.0, 2.0]


def tables():
    lobatto = np.array([-1.0, -math.sqrt(3.0 / 7.0), 0.0, math.sqrt(3.0 / 7.0), 1.0])
    weights = np.array([0.1, 49.0 / 90.0, 32.0 / 45.0, 49.0 / 90.0, 0.1])
    identity = np.eye(5)
    distance = lobatto[:, None] - lobatto[None, :] + identity
    barycentric = 1.0 / np.prod(distance, axis=1)
    derivative = (1.0 - identity) * (barycentric[None, :] / barycentric[:, None]) / distance
    legendre = np.zeros((5, 5))
    legendre[:, 0] = 1.0
    legendre[:, 1] = lobatto
    for degree in range(2, 5):
        legendre[:, degree] = (
            (2 * degree - 1) * lobatto * legendre[:, degree - 1]
            - (degree - 1) * legendre[:, degree - 2]
        ) / degree
    norms = np.array([2.0, 2.0 / 3.0, 2.0 / 5.0, 2.0 / 7.0, 0.5])
    inverse = (legendre * weights[:, None]).T / norms[:, None]
    return derivative, weights, inverse


DERIV, WEIGHTS, INVERSE = tables()
WINV = [float(1.0 / w) for w in WEIGHTS]


def inv(x):
    return pl.reciprocal(x, approx=True)


def pair_flux(l, r, n, q=None):
    gap = r[LR] - l[LR]
    square = gap * gap
    even = (r[RHO] + l[RHO]) * (0.5 + square * (-1.0 / 24.0 + square * (1.0 / 240.0)))
    mean_rho = jnp.where(square < NEAR, even, (r[RHO] - l[RHO]) * inv(gap))
    gap2 = r[LB] - l[LB]
    square2 = gap2 * gap2
    near = square2 < NEAR * 1.25 * 1.25
    c1, c2 = 2.5 / 12.0 / 1.25**2, -2.5 / 720.0 / 1.25**4
    top = jnp.where(near, 2.5 + square2 * (c1 + square2 * c2), gap2)
    thermal = top * inv(jnp.where(near, r[BE] + l[BE], r[BE] - l[BE]))
    hn, ht = (HX, HY) if n == 0 else (HY, HX)
    along = l[hn] + r[hn]
    mass = mean_rho * along
    push = l[PR] + r[PR]
    work = l[PR] * r[hn] + r[PR] * l[hn]
    dot = l[HX] * r[HX] + l[HY] * r[HY]
    if q is not None:
        mass, push, work = q * mass, q * push, q * work
    normal = mass * along + push
    tangent = mass * (l[ht] + r[ht])
    energy = mass * (dot + thermal) + work
    return (mass, normal, tangent, energy) if n == 0 else (mass, tangent, normal, energy)


def primitives_of(u):
    ri = inv(u[0])
    vx = u[1] * ri
    vy = u[2] * ri
    pressure = 0.4 * (u[3] - 0.5 * (u[1] * vx + u[2] * vy))
    beta = u[0] * inv(pressure)
    half_sound = jnp.sqrt(0.35 * pressure * ri)
    log_rho = jnp.log(u[0])
    log_beta = 1.25 * (log_rho - jnp.log(pressure))
    return (u[0], 0.5 * vx, 0.5 * vy, 0.5 * pressure, log_rho, beta, log_beta, half_sound)


def face_of(l, r, el, er, n):
    flux = pair_flux(l, r, n)
    hn = HX if n == 0 else HY
    fast = jnp.maximum(jnp.abs(l[hn]) + l[HC], jnp.abs(r[hn]) + r[HC])
    fast2 = fast + fast
    return (
        flux[0] - fast * (r[RHO] - l[RHO]),
        flux[1] - fast2 * (r[RHO] * r[HX] - l[RHO] * l[HX]),
        flux[2] - fast2 * (r[RHO] * r[HY] - l[RHO] * l[HY]),
        flux[3] + flux[3] - fast * (er - el),
    )


def transform(values):
    v0, v1, v2, v3, v4 = values
    s0, s1, d0, d1 = v0 + v4, v1 + v3, v4 - v0, v3 - v1
    out = []
    for k in range(5):
        row = [float(c) for c in INVERSE[k]]
        if k % 2 == 0:
            out.append(row[0] * s0 + row[1] * s1 + row[2] * v2)
        else:
            out.append(row[4] * d0 + row[3] * d1)
    return out


def tile(h):
    return pl.ds(pl.multiple_of(h * 8, 8), 8)


def line_terms(prim, n, node, r, u):
    def load(k):
        return [prim[q, node(k), r, :] for q in range(7)]

    acc = [[None] * 4 for _ in range(5)]
    for i in range(5):
        for j in range(i + 1, 5):
            q = float(2.0 * WEIGHTS[i] * DERIV[i, j])
            flux = pair_flux(load(i), load(j), n, q)
            for v in range(4):
                term = flux[v]
                acc[i][v] = term if acc[i][v] is None else acc[i][v] + term
                acc[j][v] = -term if acc[j][v] is None else acc[j][v] - term
    hn = HX if n == 0 else HY

    def half(k):
        c = [u[v, node(k), r, :] for v in range(4)]
        speed = prim[hn, node(k), r, :]
        p = prim[PR, node(k), r, :]
        h = [0.5 * c[1 + n], speed * c[1], speed * c[2], speed * (0.5 * c[3] + p)]
        h[1 + n] = h[1 + n] + p
        return c, h, jnp.abs(speed) + prim[HC, node(k), r, :]

    before = half(0)
    prev = None
    outs = []
    for k in range(5):
        if k < 4:
            after = half(k + 1)
            fast = jnp.maximum(before[2], after[2])
            g = [
                before[1][v] + after[1][v]
                - (fast if v < 3 else 0.5 * fast) * (after[0][v] - before[0][v])
                for v in range(4)
            ]
            before = after
        for v in range(4):
            if k == 0:
                t = g[v]
            elif k == 4:
                t = -prev[v]
            else:
                t = g[v] - prev[v]
            w = WINV[k] * ENERGY[v]
            outs.append((k, v, acc[k][v] * -w, (acc[k][v] - t) * w))
        prev = g
    return outs


def finished_column(i, rx, sx, fy, blend, sink):
    def inner(h, c):
        r = tile(h)
        share = blend[r, :]
        for k in range(5):
            m = k * 5 + i
            for v in range(4):
                rate = rx[v, m, r, :] + share * sx[v, m, r, :]
                if k == 0:
                    rate = rate + WINV[0] * fy[i, 0, v, r, :]
                if k == 4:
                    rate = rate - WINV[4] * fy[i, 1, v, r, :]
                sink(v, k, m, r, rate)
        return c

    lax.fori_loop(0, blend.shape[0] // 8, inner, 0)


def column_y(i, prim, rx, sx, fy, blend, u, sink):
    def inner(h, c):
        r = tile(h)
        share = blend[r, :]
        for k, v, vol, diff in line_terms(prim, 1, lambda k: k * 5 + i, r, u):
            m = k * 5 + i
            rate = (rx[v, m, r, :] + vol) + share * (sx[v, m, r, :] + diff)
            if k == 0:
                rate = rate + WINV[0] * fy[i, 0, v, r, :]
            if k == 4:
                rate = rate - WINV[4] * fy[i, 1, v, r, :]
            sink(v, k, m, r, rate)
        return c

    lax.fori_loop(0, blend.shape[0] // 8, inner, 0)


def volume_y(prim, rx, sx, fy, blend, u, out):
    def body(i, carry):
        def sink(v, k, m, r, rate):
            out[v, m, r, :] = rate

        column_y(i, prim, rx, sx, fy, blend, u, sink)
        return carry

    lax.fori_loop(0, 5, body, 0)


def kernel(
    ngx, ngy, state_hbm, state, prim, first, rx, sx, fy, blend, step_ref,
    rate, product, fx, raw, packx, packy, gotx, goty,
    edge, top, top_got,
    ins, hs, hr, ts, tr,
):
    loads = [
        pltpu.make_async_copy(
            state_hbm.at[:, pl.ds(a * 5, 5)], state.at[:, pl.ds(a * 5, 5)], ins.at[a]
        )
        for a in range(5)
    ]
    for copy in loads:
        copy.start()
    gx = lax.axis_index("gx")
    gy = lax.axis_index("gy")
    at_x = lambda d: (lax.rem(gx + d, ngx), gy)
    at_y = lambda d: (gx, lax.rem(gy + d, ngy))
    rows = state.shape[2]
    halves = rows // 8

    barrier = pltpu.get_barrier_semaphore()
    peers = [
        (lax.rem(gx + d // ngy, ngx), lax.rem(gy + d % ngy, ngy)) for d in range(1, ngx * ngy)
    ]
    for peer in peers:
        pl.semaphore_signal(barrier, inc=1, device_id=peer, device_id_type=MESH)

    lane = lax.broadcasted_iota(jnp.int32, (rows, LANES), 1)
    row = lax.broadcasted_iota(jnp.int32, (rows, LANES), 0)

    def remote(src, dst, send, recv, device):
        return pltpu.make_async_remote_copy(
            src_ref=src, dst_ref=dst, send_sem=send, recv_sem=recv,
            device_id=device, device_id_type=MESH,
        )

    def halo_copies(sec):
        return [
            remote(packx.at[sec, 0], gotx.at[sec, 0], hs.at[sec, 0], hr.at[sec, 0], at_x(1)),
            remote(packx.at[sec, 1], gotx.at[sec, 1], hs.at[sec, 1], hr.at[sec, 1], at_x(ngx - 1)),
            remote(packy.at[sec, 0], goty.at[sec, 0], hs.at[sec, 2], hr.at[sec, 2], at_y(1)),
            remote(packy.at[sec, 1], goty.at[sec, 1], hs.at[sec, 3], hr.at[sec, 3], at_y(ngy - 1)),
        ]

    def indicator(sec):
        def body(h, carry):
            r = tile(h)
            lines = []
            for a in range(5):
                lines.append(
                    transform(
                        [product[a * 5 + b, r, :] for b in range(5)]
                    )
                )
            sums = {}
            for l in range(5):
                modes = transform([lines[a][l] for a in range(5)])
                for k in range(5):
                    level = max(k, l)
                    sq = modes[k] * modes[k]
                    key = level if level >= 3 else 0
                    sums[key] = sums[key] + sq if key in sums else sq
            lower = sums[0] + sums[3]
            total = lower + sums[4]
            level = jnp.maximum(sums[4] / total, sums[3] / lower)
            threshold = 0.5 * 10.0 ** (-1.8 * 5.0**0.25)
            sharp = math.log((1.0 - 0.0001) / 0.0001)
            value = 1.0 / (1.0 + jnp.exp((-sharp / threshold) * (level - threshold)))
            raw[r, :] = jnp.minimum(value, 0.5)
            return carry

        lax.fori_loop(0, halves, body, 0)

    def pack(sec, u):
        hi = jnp.where(lane == 5, pltpu.roll(raw[...], 6, 1), 0.0)
        lo = jnp.where(lane == 5, pltpu.roll(raw[...], 5, 1), 0.0)
        for v in range(4):
            for a in range(5):
                k = v * 8 + a
                hi = jnp.where(lane == k, pltpu.roll(u[v, a * 5 + 4], k + 1, 1), hi)
                low = u[v, a * 5]
                lo = jnp.where(lane == k, pltpu.roll(low, k, 1) if k else low, lo)
        packx[sec, 0] = hi
        packx[sec, 1] = lo
        packy[sec] = jnp.zeros(packy.shape[1:], F32)
        for v in range(4):
            for b in range(5):
                k = v * 8 + b
                packy[sec, 0, k : k + 1, :] = u[v, 20 + b, rows - 1 : rows, :]
                packy[sec, 1, k : k + 1, :] = u[v, b, 0:1, :]
        packy[sec, 0, 5:6, :] = raw[rows - 1 : rows, :]
        packy[sec, 1, 5:6, :] = raw[0:1, :]

    def faces(u):
        def body(i, carry):
            hi, lo = i * 5 + 4, i * 5
            l = [pltpu.roll(prim[q, hi], 1, 1) for q in range(8)]
            r = [prim[q, lo] for q in range(8)]
            flux = face_of(l, r, pltpu.roll(u[3, hi], 1, 1), u[3, lo], 0)
            for v in range(4):
                fx[i, 0, v] = flux[v]
                fx[i, 1, v] = pltpu.roll(flux[v], LANES - 1, 1)
            hi, lo = 20 + i, i
            l = [pltpu.roll(prim[q, hi], 1, 0) for q in range(8)]
            r = [prim[q, lo] for q in range(8)]
            flux = face_of(l, r, pltpu.roll(u[3, hi], 1, 0), u[3, lo], 1)
            for v in range(4):
                fy[i, 0, v] = flux[v]
                fy[i, 1, v] = pltpu.roll(flux[v], rows - 1, 0)
            return carry

        lax.fori_loop(0, 5, body, 0)

    def volume_x(u):
        def body(i, carry):
            def inner(h, c):
                r = tile(h)
                for k, v, vol, diff in line_terms(prim, 0, lambda k: i * 5 + k, r, u):
                    rx[v, i * 5 + k, r, :] = vol
                    sx[v, i * 5 + k, r, :] = diff
                return c

            return lax.fori_loop(0, halves, inner, carry)

        lax.fori_loop(0, 5, body, 0)

    def finish_halo(sec):
        hi, lo = packx[sec, 0], packx[sec, 1]
        from_left, from_right = gotx[sec, 0], gotx[sec, 1]
        lslab = jnp.where(lane < 64, from_left, pltpu.roll(hi, 64, 1))
        rslab = jnp.where(lane < 64, lo, pltpu.roll(from_right, 64, 1))
        lu = [lslab if v == 0 else pltpu.roll(lslab, LANES - 8 * v, 1) for v in range(4)]
        ru = [rslab if v == 0 else pltpu.roll(rslab, LANES - 8 * v, 1) for v in range(4)]
        flux = face_of(primitives_of(lu), primitives_of(ru), lu[3], ru[3], 0)
        for a in range(5):
            for v in range(4):
                low = pltpu.roll(flux[v], LANES - a, 1) if a else flux[v]
                high = pltpu.roll(flux[v], 63 - a, 1)
                flo = jnp.where(lane == 0, low, fx[a, 0, v])
                fhi = jnp.where(lane == LANES - 1, high, fx[a, 1, v])
                rx[v, a * 5] = rx[v, a * 5] + WINV[0] * flo
                rx[v, a * 5 + 4] = rx[v, a * 5 + 4] - WINV[4] * fhi
        for side in range(2):
            lsrc = goty.at[sec, 0] if side == 0 else packy.at[sec, 0]
            rsrc = packy.at[sec, 1] if side == 0 else goty.at[sec, 1]
            lu = [lsrc[8 * v : 8 * v + 8, :] for v in range(4)]
            ru = [rsrc[8 * v : 8 * v + 8, :] for v in range(4)]
            flux = face_of(primitives_of(lu), primitives_of(ru), lu[3], ru[3], 1)
            for v in range(4):
                edge[side, v] = flux[v]
        for b in range(5):
            for v in range(4):
                fy[b, 0, v, 0:1, :] = edge[0, v, b : b + 1, :]
                fy[b, 1, v, rows - 1 : rows, :] = edge[1, v, b : b + 1, :]
        own = raw[...]
        left = jnp.where(lane == 0, pltpu.roll(from_left, LANES - 5, 1), pltpu.roll(own, 1, 1))
        right = jnp.where(
            lane == LANES - 1, pltpu.roll(from_right, LANES - 6, 1), pltpu.roll(own, LANES - 1, 1)
        )
        below = jnp.where(row == 0, goty[sec, 0, 5:6, :], pltpu.roll(own, 1, 0))
        above = jnp.where(row == rows - 1, goty[sec, 1, 5:6, :], pltpu.roll(own, rows - 1, 0))
        beside = jnp.maximum(jnp.maximum(left, right), jnp.maximum(below, above))
        blend[...] = jnp.maximum(own, 0.5 * beside)

    def early_column(i, carry):
        def inner(h, c):
            r = tile(h)
            for k, v, vol, diff in line_terms(prim, 1, lambda k: k * 5 + i, r, first):
                m = k * 5 + i
                rx[v, m, r, :] = rx[v, m, r, :] + vol
                sx[v, m, r, :] = sx[v, m, r, :] + diff
            return c

        return lax.fori_loop(0, halves, inner, carry)

    def prepare(a, fastest):
        for m in [a * 5 + b for b in range(5)]:
            q = primitives_of([state[v, m] for v in range(4)])
            for f in range(8):
                prim[f, m] = q[f]
            product[m] = q[RHO] * q[PR]
            speed = jnp.sqrt(q[HX] * q[HX] + q[HY] * q[HY]) + q[HC]
            fastest = jnp.maximum(fastest, speed)
        return fastest

    def load_and_prepare(a, fastest):
        pltpu.make_async_copy(
            state_hbm.at[:, pl.ds(a * 5, 5)], state.at[:, pl.ds(a * 5, 5)], ins.at[a]
        ).wait()
        return prepare(a, fastest)

    fastest = lax.fori_loop(0, 5, load_and_prepare, jnp.zeros((rows, LANES), F32))
    local_top = fastest[0:8]
    for h in range(1, halves):
        local_top = jnp.maximum(local_top, fastest[8 * h : 8 * h + 8])
    top[...] = jnp.broadcast_to(jnp.max(local_top, axis=0, keepdims=True), (8, LANES))
    indicator(0)
    pack(0, state)
    pl.semaphore_wait(barrier, ngx * ngy - 1)
    for d, peer in enumerate(peers):
        remote(
            top.at[pl.ds(0, 1)], top_got.at[d, pl.ds(0, 1)], ts.at[0], tr.at[0], peer
        ).start()
    halos = halo_copies(0)
    for copy in halos:
        copy.start()
    faces(state)
    volume_x(state)
    for copy in halos:
        copy.wait()
    finish_halo(0)
    volume_y(prim, rx, sx, fy, blend, state, rate)
    every = top_got.at[:, pl.ds(0, 1)]
    tops = remote(every, every, ts.at[0], tr.at[0], peers[0])
    tops.wait_recv()
    best = top[0:1, :]
    for d in range(len(peers)):
        best = jnp.maximum(best, top_got[d, 0:1, :])
    step = (COURANT * 2.0 / 9.0) / (2.0 * jnp.max(best, axis=1, keepdims=True))
    step = jnp.broadcast_to(step, (8, LANES))
    step_full = jnp.concatenate([step] * halves, axis=0)

    def advance(a, carry):
        for m in [a * 5 + b for b in range(5)]:
            u = [state[v, m] + step_full * rate[v, m] for v in range(4)]
            for v in range(4):
                first[v, m] = u[v]
            product[m] = u[0] * u[3] - 0.5 * (u[1] * u[1] + u[2] * u[2])
        return carry

    lax.fori_loop(0, 5, advance, 0)
    indicator(1)
    pack(1, first)
    halos = halo_copies(1)
    for copy in halos:
        copy.start()
    step_ref[...] = step

    def prepare2(a, carry):
        for m in [a * 5 + b for b in range(5)]:
            q = primitives_of([first[v, m] for v in range(4)])
            for f in range(8):
                prim[f, m] = q[f]
        return carry

    lax.fori_loop(0, 5, prepare2, 0)
    faces(first)
    volume_x(first)
    lax.fori_loop(0, EARLY, early_column, 0)
    tops.wait_send()
    for copy in halos:
        copy.wait()
    finish_halo(1)


def last_kernel(state, prim, first, rx, sx, fy, blend, step_ref, adv, tend, adv_v, tend_v, sems):
    step = step_ref[...]

    def column(i):
        pairs = ((adv_v, adv), (tend_v, tend))
        return [
            pltpu.make_async_copy(src.at[i], dst.at[:, :, i], sems.at[k, i])
            for k, (src, dst) in enumerate(pairs)
        ]

    def body(early, i, carry):
        def sink(v, k, m, r, rate):
            tend_v[i, v, k, r, :] = rate
            adv_v[i, v, k, r, :] = 0.5 * state[v, m, r, :] + 0.5 * (
                first[v, m, r, :] + step * rate
            )

        if early:
            finished_column(i, rx, sx, fy, blend, sink)
        else:
            column_y(i, prim, rx, sx, fy, blend, first, sink)
        for copy in column(i):
            copy.start()
        return carry

    lax.fori_loop(0, EARLY, functools.partial(body, True), 0)
    lax.fori_loop(EARLY, 5, functools.partial(body, False), 0)
    for i in range(5):
        for copy in column(i):
            copy.wait()


def local(ngx, ngy, state):
    shape = state.shape
    rows, cols = shape[3], shape[4]
    flat = (4, 25, rows, cols)
    vmem = lambda *s: pltpu.VMEM(s, F32)
    whole = pl.BlockSpec(memory_space=pltpu.VMEM)
    hbm = pl.BlockSpec(memory_space=pltpu.HBM)
    mid = [flat, (8, 25, rows, cols), flat, flat, flat, (5, 2, 4, rows, cols), (rows, cols), (8, cols)]
    kept = pl.pallas_call(
        functools.partial(kernel, ngx, ngy),
        out_shape=[jax.ShapeDtypeStruct(m, F32) for m in mid],
        in_specs=[hbm],
        out_specs=[whole] * len(mid),
        scratch_shapes=[
            vmem(*flat), vmem(25, rows, cols), vmem(5, 2, 4, rows, cols), vmem(rows, cols),
            vmem(2, 2, rows, cols), vmem(2, 2, 32, cols),
            vmem(2, 2, rows, cols), vmem(2, 2, 32, cols),
            vmem(2, 4, 8, cols),
            vmem(8, cols), vmem(ngx * ngy - 1, 8, cols),
            pltpu.SemaphoreType.DMA((5,)),
            pltpu.SemaphoreType.DMA((2, 4)), pltpu.SemaphoreType.DMA((2, 4)),
            pltpu.SemaphoreType.DMA((1,)), pltpu.SemaphoreType.DMA((1,)),
        ],
        compiler_params=pltpu.CompilerParams(collective_id=0, has_side_effects=True,
                                             vmem_limit_bytes=16 * 1024 * 1024),
        name="dg_sections",
    )(pltpu.with_memory_space_constraint(state.reshape(flat), pltpu.HBM))
    return pl.pallas_call(
        last_kernel,
        out_shape=(jax.ShapeDtypeStruct(shape, F32),) * 2,
        in_specs=[whole] * len(mid),
        out_specs=[hbm] * 2,
        scratch_shapes=[
            vmem(5, 4, 5, rows, cols), vmem(5, 4, 5, rows, cols), pltpu.SemaphoreType.DMA((2, 5))
        ],
        compiler_params=pltpu.CompilerParams(vmem_limit_bytes=16 * 1024 * 1024),
        name="dg_last_pass",
    )(*kept)


def solution(mesh):
    spec = P(None, None, None, "gy", "gx")
    return jax.shard_map(
        functools.partial(local, mesh.shape["gx"], mesh.shape["gy"]),
        mesh=mesh,
        in_specs=(spec,),
        out_specs=(spec, spec),
        check_vma=False,
    )
```

```python
import functools
import math

import jax
import jax.numpy as jnp
import numpy as np
from jax import lax
from jax.experimental import pallas as pl
from jax.experimental.pallas import tpu as pltpu
from jax.sharding import PartitionSpec as P

MESH = pl.DeviceIdType.MESH
COURANT = 0.2
F32 = jnp.float32
LANES = 128
RHO, HX, HY, PR, LR, BE, LB, HC = range(8)
NEAR = 1.0 / 64.0
EARLY = 4
ENERGY = [1.0, 1.0, 1.0, 2.0]


def tables():
    lobatto = np.array([-1.0, -math.sqrt(3.0 / 7.0), 0.0, math.sqrt(3.0 / 7.0), 1.0])
    weights = np.array([0.1, 49.0 / 90.0, 32.0 / 45.0, 49.0 / 90.0, 0.1])
    identity = np.eye(5)
    distance = lobatto[:, None] - lobatto[None, :] + identity
    barycentric = 1.0 / np.prod(distance, axis=1)
    derivative = (1.0 - identity) * (barycentric[None, :] / barycentric[:, None]) / distance
    legendre = np.zeros((5, 5))
    legendre[:, 0] = 1.0
    legendre[:, 1] = lobatto
    for degree in range(2, 5):
        legendre[:, degree] = (
            (2 * degree - 1) * lobatto * legendre[:, degree - 1]
            - (degree - 1) * legendre[:, degree - 2]
        ) / degree
    norms = np.array([2.0, 2.0 / 3.0, 2.0 / 5.0, 2.0 / 7.0, 0.5])
    inverse = (legendre * weights[:, None]).T / norms[:, None]
    return derivative, weights, inverse


DERIV, WEIGHTS, INVERSE = tables()
WINV = [float(1.0 / w) for w in WEIGHTS]


def inv(x):
    return pl.reciprocal(x, approx=True)


def pair_flux(l, r, n, q=None):
    gap = r[LR] - l[LR]
    square = gap * gap
    even = (r[RHO] + l[RHO]) * (0.5 + square * (-1.0 / 24.0 + square * (1.0 / 240.0)))
    mean_rho = jnp.where(square < NEAR, even, (r[RHO] - l[RHO]) * inv(gap))
    gap2 = r[LB] - l[LB]
    square2 = gap2 * gap2
    near = square2 < NEAR * 1.25 * 1.25
    c1, c2 = 2.5 / 12.0 / 1.25**2, -2.5 / 720.0 / 1.25**4
    top = jnp.where(near, 2.5 + square2 * (c1 + square2 * c2), gap2)
    thermal = top * inv(jnp.where(near, r[BE] + l[BE], r[BE] - l[BE]))
    hn, ht = (HX, HY) if n == 0 else (HY, HX)
    along = l[hn] + r[hn]
    mass = mean_rho * along
    push = l[PR] + r[PR]
    work = l[PR] * r[hn] + r[PR] * l[hn]
    dot = l[HX] * r[HX] + l[HY] * r[HY]
    if q is not None:
        mass, push, work = q * mass, q * push, q * work
    normal = mass * along + push
    tangent = mass * (l[ht] + r[ht])
    energy = mass * (dot + thermal) + work
    return (mass, normal, tangent, energy) if n == 0 else (mass, tangent, normal, energy)


def primitives_of(u):
    ri = inv(u[0])
    vx = u[1] * ri
    vy = u[2] * ri
    pressure = 0.4 * (u[3] - 0.5 * (u[1] * vx + u[2] * vy))
    beta = u[0] * inv(pressure)
    half_sound = jnp.sqrt(0.35 * pressure * ri)
    log_rho = jnp.log(u[0])
    log_beta = 1.25 * (log_rho - jnp.log(pressure))
    return (u[0], 0.5 * vx, 0.5 * vy, 0.5 * pressure, log_rho, beta, log_beta, half_sound)


def face_of(l, r, el, er, n):
    flux = pair_flux(l, r, n)
    hn = HX if n == 0 else HY
    fast = jnp.maximum(jnp.abs(l[hn]) + l[HC], jnp.abs(r[hn]) + r[HC])
    fast2 = fast + fast
    return (
        flux[0] - fast * (r[RHO] - l[RHO]),
        flux[1] - fast2 * (r[RHO] * r[HX] - l[RHO] * l[HX]),
        flux[2] - fast2 * (r[RHO] * r[HY] - l[RHO] * l[HY]),
        flux[3] + flux[3] - fast * (er - el),
    )


def transform(values):
    v0, v1, v2, v3, v4 = values
    s0, s1, d0, d1 = v0 + v4, v1 + v3, v4 - v0, v3 - v1
    out = []
    for k in range(5):
        row = [float(c) for c in INVERSE[k]]
        if k % 2 == 0:
            out.append(row[0] * s0 + row[1] * s1 + row[2] * v2)
        else:
            out.append(row[4] * d0 + row[3] * d1)
    return out


def tile(h):
    return pl.ds(pl.multiple_of(h * 8, 8), 8)


def line_terms(prim, n, node, r, u):
    def load(k):
        return [prim[q, node(k), r, :] for q in range(7)]

    acc = [[None] * 4 for _ in range(5)]
    for i in range(5):
        for j in range(i + 1, 5):
            q = float(2.0 * WEIGHTS[i] * DERIV[i, j])
            flux = pair_flux(load(i), load(j), n, q)
            for v in range(4):
                term = flux[v]
                acc[i][v] = term if acc[i][v] is None else acc[i][v] + term
                acc[j][v] = -term if acc[j][v] is None else acc[j][v] - term
    hn = HX if n == 0 else HY

    def half(k):
        c = [u[v, node(k), r, :] for v in range(4)]
        speed = prim[hn, node(k), r, :]
        p = prim[PR, node(k), r, :]
        h = [0.5 * c[1 + n], speed * c[1], speed * c[2], speed * (0.5 * c[3] + p)]
        h[1 + n] = h[1 + n] + p
        return c, h, jnp.abs(speed) + prim[HC, node(k), r, :]

    before = half(0)
    prev = None
    outs = []
    for k in range(5):
        if k < 4:
            after = half(k + 1)
            fast = jnp.maximum(before[2], after[2])
            g = [
                before[1][v] + after[1][v]
                - (fast if v < 3 else 0.5 * fast) * (after[0][v] - before[0][v])
                for v in range(4)
            ]
            before = after
        for v in range(4):
            if k == 0:
                t = g[v]
            elif k == 4:
                t = -prev[v]
            else:
                t = g[v] - prev[v]
            w = WINV[k] * ENERGY[v]
            outs.append((k, v, acc[k][v] * -w, (acc[k][v] - t) * w))
        prev = g
    return outs


def finished_column(i, rx, sx, fy, blend, sink):
    def inner(h, c):
        r = tile(h)
        share = blend[r, :]
        for k in range(5):
            m = k * 5 + i
            for v in range(4):
                rate = rx[v, m, r, :] + share * sx[v, m, r, :]
                if k == 0:
                    rate = rate + WINV[0] * fy[i, 0, v, r, :]
                if k == 4:
                    rate = rate - WINV[4] * fy[i, 1, v, r, :]
                sink(v, k, m, r, rate)
        return c

    lax.fori_loop(0, blend.shape[0] // 8, inner, 0)


def column_y(i, prim, rx, sx, fy, blend, u, sink):
    def inner(h, c):
        r = tile(h)
        share = blend[r, :]
        for k, v, vol, diff in line_terms(prim, 1, lambda k: k * 5 + i, r, u):
            m = k * 5 + i
            rate = (rx[v, m, r, :] + vol) + share * (sx[v, m, r, :] + diff)
            if k == 0:
                rate = rate + WINV[0] * fy[i, 0, v, r, :]
            if k == 4:
                rate = rate - WINV[4] * fy[i, 1, v, r, :]
            sink(v, k, m, r, rate)
        return c

    lax.fori_loop(0, blend.shape[0] // 8, inner, 0)


def volume_y(prim, rx, sx, fy, blend, u, out):
    def body(early, i, carry):
        def sink(v, k, m, r, rate):
            out[v, m, r, :] = rate

        if early:
            finished_column(i, rx, sx, fy, blend, sink)
        else:
            column_y(i, prim, rx, sx, fy, blend, u, sink)
        return carry

    lax.fori_loop(0, EARLY, functools.partial(body, True), 0)
    lax.fori_loop(EARLY, 5, functools.partial(body, False), 0)


def kernel(
    ngx, ngy, state_hbm, state, prim, first, rx, sx, fy, blend, step_ref,
    rate, product, fx, raw, packx, packy, gotx, goty,
    edge, top, top_got,
    ins, hs, hr, ts, tr,
):
    loads = [
        pltpu.make_async_copy(
            state_hbm.at[:, pl.ds(a * 5, 5)], state.at[:, pl.ds(a * 5, 5)], ins.at[a]
        )
        for a in range(5)
    ]
    for copy in loads:
        copy.start()
    gx = lax.axis_index("gx")
    gy = lax.axis_index("gy")
    at_x = lambda d: (lax.rem(gx + d, ngx), gy)
    at_y = lambda d: (gx, lax.rem(gy + d, ngy))
    rows = state.shape[2]
    halves = rows // 8

    barrier = pltpu.get_barrier_semaphore()
    peers = [
        (lax.rem(gx + d // ngy, ngx), lax.rem(gy + d % ngy, ngy)) for d in range(1, ngx * ngy)
    ]
    for peer in peers:
        pl.semaphore_signal(barrier, inc=1, device_id=peer, device_id_type=MESH)

    lane = lax.broadcasted_iota(jnp.int32, (rows, LANES), 1)
    row = lax.broadcasted_iota(jnp.int32, (rows, LANES), 0)

    def remote(src, dst, send, recv, device):
        return pltpu.make_async_remote_copy(
            src_ref=src, dst_ref=dst, send_sem=send, recv_sem=recv,
            device_id=device, device_id_type=MESH,
        )

    def halo_copies(sec):
        return [
            remote(packx.at[sec, 0], gotx.at[sec, 0], hs.at[sec, 0], hr.at[sec, 0], at_x(1)),
            remote(packx.at[sec, 1], gotx.at[sec, 1], hs.at[sec, 1], hr.at[sec, 1], at_x(ngx - 1)),
            remote(packy.at[sec, 0], goty.at[sec, 0], hs.at[sec, 2], hr.at[sec, 2], at_y(1)),
            remote(packy.at[sec, 1], goty.at[sec, 1], hs.at[sec, 3], hr.at[sec, 3], at_y(ngy - 1)),
        ]

    def indicator(sec):
        def body(h, carry):
            r = tile(h)
            lines = []
            for a in range(5):
                lines.append(
                    transform(
                        [product[a * 5 + b, r, :] for b in range(5)]
                    )
                )
            sums = {}
            for l in range(5):
                modes = transform([lines[a][l] for a in range(5)])
                for k in range(5):
                    level = max(k, l)
                    sq = modes[k] * modes[k]
                    key = level if level >= 3 else 0
                    sums[key] = sums[key] + sq if key in sums else sq
            lower = sums[0] + sums[3]
            total = lower + sums[4]
            level = jnp.maximum(sums[4] / total, sums[3] / lower)
            threshold = 0.5 * 10.0 ** (-1.8 * 5.0**0.25)
            sharp = math.log((1.0 - 0.0001) / 0.0001)
            value = 1.0 / (1.0 + jnp.exp((-sharp / threshold) * (level - threshold)))
            raw[r, :] = jnp.minimum(value, 0.5)
            return carry

        lax.fori_loop(0, halves, body, 0)

    def pack(sec, u):
        hi = jnp.where(lane == 5, pltpu.roll(raw[...], 6, 1), 0.0)
        lo = jnp.where(lane == 5, pltpu.roll(raw[...], 5, 1), 0.0)
        for v in range(4):
            for a in range(5):
                k = v * 8 + a
                hi = jnp.where(lane == k, pltpu.roll(u[v, a * 5 + 4], k + 1, 1), hi)
                low = u[v, a * 5]
                lo = jnp.where(lane == k, pltpu.roll(low, k, 1) if k else low, lo)
        packx[sec, 0] = hi
        packx[sec, 1] = lo
        packy[sec] = jnp.zeros(packy.shape[1:], F32)
        for v in range(4):
            for b in range(5):
                k = v * 8 + b
                packy[sec, 0, k : k + 1, :] = u[v, 20 + b, rows - 1 : rows, :]
                packy[sec, 1, k : k + 1, :] = u[v, b, 0:1, :]
        packy[sec, 0, 5:6, :] = raw[rows - 1 : rows, :]
        packy[sec, 1, 5:6, :] = raw[0:1, :]

    def faces(u):
        def body(i, carry):
            hi, lo = i * 5 + 4, i * 5
            l = [pltpu.roll(prim[q, hi], 1, 1) for q in range(8)]
            r = [prim[q, lo] for q in range(8)]
            flux = face_of(l, r, pltpu.roll(u[3, hi], 1, 1), u[3, lo], 0)
            for v in range(4):
                fx[i, 0, v] = flux[v]
                fx[i, 1, v] = pltpu.roll(flux[v], LANES - 1, 1)
            hi, lo = 20 + i, i
            l = [pltpu.roll(prim[q, hi], 1, 0) for q in range(8)]
            r = [prim[q, lo] for q in range(8)]
            flux = face_of(l, r, pltpu.roll(u[3, hi], 1, 0), u[3, lo], 1)
            for v in range(4):
                fy[i, 0, v] = flux[v]
                fy[i, 1, v] = pltpu.roll(flux[v], rows - 1, 0)
            return carry

        lax.fori_loop(0, 5, body, 0)

    def volume_x(u):
        def body(i, carry):
            def inner(h, c):
                r = tile(h)
                for k, v, vol, diff in line_terms(prim, 0, lambda k: i * 5 + k, r, u):
                    rx[v, i * 5 + k, r, :] = vol
                    sx[v, i * 5 + k, r, :] = diff
                return c

            return lax.fori_loop(0, halves, inner, carry)

        lax.fori_loop(0, 5, body, 0)

    def finish_halo(sec):
        hi, lo = packx[sec, 0], packx[sec, 1]
        from_left, from_right = gotx[sec, 0], gotx[sec, 1]
        lslab = jnp.where(lane < 64, from_left, pltpu.roll(hi, 64, 1))
        rslab = jnp.where(lane < 64, lo, pltpu.roll(from_right, 64, 1))
        lu = [lslab if v == 0 else pltpu.roll(lslab, LANES - 8 * v, 1) for v in range(4)]
        ru = [rslab if v == 0 else pltpu.roll(rslab, LANES - 8 * v, 1) for v in range(4)]
        flux = face_of(primitives_of(lu), primitives_of(ru), lu[3], ru[3], 0)
        for a in range(5):
            for v in range(4):
                low = pltpu.roll(flux[v], LANES - a, 1) if a else flux[v]
                high = pltpu.roll(flux[v], 63 - a, 1)
                flo = jnp.where(lane == 0, low, fx[a, 0, v])
                fhi = jnp.where(lane == LANES - 1, high, fx[a, 1, v])
                rx[v, a * 5] = rx[v, a * 5] + WINV[0] * flo
                rx[v, a * 5 + 4] = rx[v, a * 5 + 4] - WINV[4] * fhi
        for side in range(2):
            lsrc = goty.at[sec, 0] if side == 0 else packy.at[sec, 0]
            rsrc = packy.at[sec, 1] if side == 0 else goty.at[sec, 1]
            lu = [lsrc[8 * v : 8 * v + 8, :] for v in range(4)]
            ru = [rsrc[8 * v : 8 * v + 8, :] for v in range(4)]
            flux = face_of(primitives_of(lu), primitives_of(ru), lu[3], ru[3], 1)
            for v in range(4):
                edge[side, v] = flux[v]
        for b in range(5):
            for v in range(4):
                fy[b, 0, v, 0:1, :] = edge[0, v, b : b + 1, :]
                fy[b, 1, v, rows - 1 : rows, :] = edge[1, v, b : b + 1, :]
        own = raw[...]
        left = jnp.where(lane == 0, pltpu.roll(from_left, LANES - 5, 1), pltpu.roll(own, 1, 1))
        right = jnp.where(
            lane == LANES - 1, pltpu.roll(from_right, LANES - 6, 1), pltpu.roll(own, LANES - 1, 1)
        )
        below = jnp.where(row == 0, goty[sec, 0, 5:6, :], pltpu.roll(own, 1, 0))
        above = jnp.where(row == rows - 1, goty[sec, 1, 5:6, :], pltpu.roll(own, rows - 1, 0))
        beside = jnp.maximum(jnp.maximum(left, right), jnp.maximum(below, above))
        blend[...] = jnp.maximum(own, 0.5 * beside)

    def early_column(u, i, carry):
        def inner(h, c):
            r = tile(h)
            for k, v, vol, diff in line_terms(prim, 1, lambda k: k * 5 + i, r, u):
                m = k * 5 + i
                rx[v, m, r, :] = rx[v, m, r, :] + vol
                sx[v, m, r, :] = sx[v, m, r, :] + diff
            return c

        return lax.fori_loop(0, halves, inner, carry)

    def prepare(a, fastest):
        for m in [a * 5 + b for b in range(5)]:
            q = primitives_of([state[v, m] for v in range(4)])
            for f in range(8):
                prim[f, m] = q[f]
            product[m] = q[RHO] * q[PR]
            speed = jnp.sqrt(q[HX] * q[HX] + q[HY] * q[HY]) + q[HC]
            fastest = jnp.maximum(fastest, speed)
        return fastest

    def load_and_prepare(a, fastest):
        pltpu.make_async_copy(
            state_hbm.at[:, pl.ds(a * 5, 5)], state.at[:, pl.ds(a * 5, 5)], ins.at[a]
        ).wait()
        return prepare(a, fastest)

    fastest = lax.fori_loop(0, 5, load_and_prepare, jnp.zeros((rows, LANES), F32))
    local_top = fastest[0:8]
    for h in range(1, halves):
        local_top = jnp.maximum(local_top, fastest[8 * h : 8 * h + 8])
    top[...] = jnp.broadcast_to(jnp.max(local_top, axis=0, keepdims=True), (8, LANES))
    indicator(0)
    pack(0, state)
    pl.semaphore_wait(barrier, ngx * ngy - 1)
    for d, peer in enumerate(peers):
        remote(
            top.at[pl.ds(0, 1)], top_got.at[d, pl.ds(0, 1)], ts.at[0], tr.at[0], peer
        ).start()
    halos = halo_copies(0)
    for copy in halos:
        copy.start()
    faces(state)
    volume_x(state)
    lax.fori_loop(0, EARLY, functools.partial(early_column, state), 0)
    for copy in halos:
        copy.wait()
    finish_halo(0)
    volume_y(prim, rx, sx, fy, blend, state, rate)
    every = top_got.at[:, pl.ds(0, 1)]
    tops = remote(every, every, ts.at[0], tr.at[0], peers[0])
    tops.wait_recv()
    best = top[0:1, :]
    for d in range(len(peers)):
        best = jnp.maximum(best, top_got[d, 0:1, :])
    step = (COURANT * 2.0 / 9.0) / (2.0 * jnp.max(best, axis=1, keepdims=True))
    step = jnp.broadcast_to(step, (8, LANES))
    step_full = jnp.concatenate([step] * halves, axis=0)

    def advance(a, carry):
        for m in [a * 5 + b for b in range(5)]:
            u = [state[v, m] + step_full * rate[v, m] for v in range(4)]
            for v in range(4):
                first[v, m] = u[v]
            product[m] = u[0] * u[3] - 0.5 * (u[1] * u[1] + u[2] * u[2])
        return carry

    lax.fori_loop(0, 5, advance, 0)
    indicator(1)
    pack(1, first)
    halos = halo_copies(1)
    for copy in halos:
        copy.start()
    step_ref[...] = step

    def prepare2(a, carry):
        for m in [a * 5 + b for b in range(5)]:
            q = primitives_of([first[v, m] for v in range(4)])
            for f in range(8):
                prim[f, m] = q[f]
        return carry

    lax.fori_loop(0, 5, prepare2, 0)
    faces(first)
    volume_x(first)
    lax.fori_loop(0, EARLY, functools.partial(early_column, first), 0)
    tops.wait_send()
    for copy in halos:
        copy.wait()
    finish_halo(1)


def last_kernel(state, prim, first, rx, sx, fy, blend, step_ref, adv, tend, adv_v, tend_v, sems):
    step = step_ref[...]

    def column(i):
        pairs = ((adv_v, adv), (tend_v, tend))
        return [
            pltpu.make_async_copy(src.at[i], dst.at[:, :, i], sems.at[k, i])
            for k, (src, dst) in enumerate(pairs)
        ]

    def body(early, i, carry):
        def sink(v, k, m, r, rate):
            tend_v[i, v, k, r, :] = rate
            adv_v[i, v, k, r, :] = 0.5 * state[v, m, r, :] + 0.5 * (
                first[v, m, r, :] + step * rate
            )

        if early:
            finished_column(i, rx, sx, fy, blend, sink)
        else:
            column_y(i, prim, rx, sx, fy, blend, first, sink)
        for copy in column(i):
            copy.start()
        return carry

    lax.fori_loop(0, EARLY, functools.partial(body, True), 0)
    lax.fori_loop(EARLY, 5, functools.partial(body, False), 0)
    for i in range(5):
        for copy in column(i):
            copy.wait()


def local(ngx, ngy, state):
    shape = state.shape
    rows, cols = shape[3], shape[4]
    flat = (4, 25, rows, cols)
    vmem = lambda *s: pltpu.VMEM(s, F32)
    whole = pl.BlockSpec(memory_space=pltpu.VMEM)
    hbm = pl.BlockSpec(memory_space=pltpu.HBM)
    mid = [flat, (8, 25, rows, cols), flat, flat, flat, (5, 2, 4, rows, cols), (rows, cols), (8, cols)]
    kept = pl.pallas_call(
        functools.partial(kernel, ngx, ngy),
        out_shape=[jax.ShapeDtypeStruct(m, F32) for m in mid],
        in_specs=[hbm],
        out_specs=[whole] * len(mid),
        scratch_shapes=[
            vmem(*flat), vmem(25, rows, cols), vmem(5, 2, 4, rows, cols), vmem(rows, cols),
            vmem(2, 2, rows, cols), vmem(2, 2, 32, cols),
            vmem(2, 2, rows, cols), vmem(2, 2, 32, cols),
            vmem(2, 4, 8, cols),
            vmem(8, cols), vmem(ngx * ngy - 1, 8, cols),
            pltpu.SemaphoreType.DMA((5,)),
            pltpu.SemaphoreType.DMA((2, 4)), pltpu.SemaphoreType.DMA((2, 4)),
            pltpu.SemaphoreType.DMA((1,)), pltpu.SemaphoreType.DMA((1,)),
        ],
        compiler_params=pltpu.CompilerParams(collective_id=0, has_side_effects=True,
                                             vmem_limit_bytes=16 * 1024 * 1024),
        name="dg_sections",
    )(pltpu.with_memory_space_constraint(state.reshape(flat), pltpu.HBM))
    return pl.pallas_call(
        last_kernel,
        out_shape=(jax.ShapeDtypeStruct(shape, F32),) * 2,
        in_specs=[whole] * len(mid),
        out_specs=[hbm] * 2,
        scratch_shapes=[
            vmem(5, 4, 5, rows, cols), vmem(5, 4, 5, rows, cols), pltpu.SemaphoreType.DMA((2, 5))
        ],
        compiler_params=pltpu.CompilerParams(vmem_limit_bytes=16 * 1024 * 1024),
        name="dg_last_pass",
    )(*kept)


def solution(mesh):
    spec = P(None, None, None, "gy", "gx")
    return jax.shard_map(
        functools.partial(local, mesh.shape["gx"], mesh.shape["gy"]),
        mesh=mesh,
        in_specs=(spec,),
        out_specs=(spec, spec),
        check_vma=False,
    )
```

```python
import functools
import math

import jax
import jax.numpy as jnp
import numpy as np
from jax import lax
from jax.experimental import pallas as pl
from jax.experimental.pallas import tpu as pltpu
from jax.sharding import PartitionSpec as P

MESH = pl.DeviceIdType.MESH
COURANT = 0.2
F32 = jnp.float32
LANES = 128
RHO, HX, HY, PR, LR, BE, LB, HC = range(8)
NEAR = 1.0 / 64.0
EARLY = 5
ENERGY = [1.0, 1.0, 1.0, 2.0]


def tables():
    lobatto = np.array([-1.0, -math.sqrt(3.0 / 7.0), 0.0, math.sqrt(3.0 / 7.0), 1.0])
    weights = np.array([0.1, 49.0 / 90.0, 32.0 / 45.0, 49.0 / 90.0, 0.1])
    identity = np.eye(5)
    distance = lobatto[:, None] - lobatto[None, :] + identity
    barycentric = 1.0 / np.prod(distance, axis=1)
    derivative = (1.0 - identity) * (barycentric[None, :] / barycentric[:, None]) / distance
    legendre = np.zeros((5, 5))
    legendre[:, 0] = 1.0
    legendre[:, 1] = lobatto
    for degree in range(2, 5):
        legendre[:, degree] = (
            (2 * degree - 1) * lobatto * legendre[:, degree - 1]
            - (degree - 1) * legendre[:, degree - 2]
        ) / degree
    norms = np.array([2.0, 2.0 / 3.0, 2.0 / 5.0, 2.0 / 7.0, 0.5])
    inverse = (legendre * weights[:, None]).T / norms[:, None]
    return derivative, weights, inverse


DERIV, WEIGHTS, INVERSE = tables()
WINV = [float(1.0 / w) for w in WEIGHTS]


def inv(x):
    return pl.reciprocal(x, approx=True)


def pair_flux(l, r, n, q=None):
    gap = r[LR] - l[LR]
    square = gap * gap
    even = (r[RHO] + l[RHO]) * (0.5 + square * (-1.0 / 24.0 + square * (1.0 / 240.0)))
    mean_rho = jnp.where(square < NEAR, even, (r[RHO] - l[RHO]) * inv(gap))
    gap2 = r[LB] - l[LB]
    square2 = gap2 * gap2
    near = square2 < NEAR * 1.25 * 1.25
    c1, c2 = 2.5 / 12.0 / 1.25**2, -2.5 / 720.0 / 1.25**4
    top = jnp.where(near, 2.5 + square2 * (c1 + square2 * c2), gap2)
    thermal = top * inv(jnp.where(near, r[BE] + l[BE], r[BE] - l[BE]))
    hn, ht = (HX, HY) if n == 0 else (HY, HX)
    along = l[hn] + r[hn]
    mass = mean_rho * along
    push = l[PR] + r[PR]
    work = l[PR] * r[hn] + r[PR] * l[hn]
    dot = l[HX] * r[HX] + l[HY] * r[HY]
    if q is not None:
        mass, push, work = q * mass, q * push, q * work
    normal = mass * along + push
    tangent = mass * (l[ht] + r[ht])
    energy = mass * (dot + thermal) + work
    return (mass, normal, tangent, energy) if n == 0 else (mass, tangent, normal, energy)


def primitives_of(u):
    ri = inv(u[0])
    vx = u[1] * ri
    vy = u[2] * ri
    pressure = 0.4 * (u[3] - 0.5 * (u[1] * vx + u[2] * vy))
    beta = u[0] * inv(pressure)
    half_sound = jnp.sqrt(0.35 * pressure * ri)
    log_rho = jnp.log(u[0])
    log_beta = 1.25 * (log_rho - jnp.log(pressure))
    return (u[0], 0.5 * vx, 0.5 * vy, 0.5 * pressure, log_rho, beta, log_beta, half_sound)


def face_of(l, r, el, er, n):
    flux = pair_flux(l, r, n)
    hn = HX if n == 0 else HY
    fast = jnp.maximum(jnp.abs(l[hn]) + l[HC], jnp.abs(r[hn]) + r[HC])
    fast2 = fast + fast
    return (
        flux[0] - fast * (r[RHO] - l[RHO]),
        flux[1] - fast2 * (r[RHO] * r[HX] - l[RHO] * l[HX]),
        flux[2] - fast2 * (r[RHO] * r[HY] - l[RHO] * l[HY]),
        flux[3] + flux[3] - fast * (er - el),
    )


def transform(values):
    v0, v1, v2, v3, v4 = values
    s0, s1, d0, d1 = v0 + v4, v1 + v3, v4 - v0, v3 - v1
    out = []
    for k in range(5):
        row = [float(c) for c in INVERSE[k]]
        if k % 2 == 0:
            out.append(row[0] * s0 + row[1] * s1 + row[2] * v2)
        else:
            out.append(row[4] * d0 + row[3] * d1)
    return out


def tile(h):
    return pl.ds(pl.multiple_of(h * 8, 8), 8)


def line_terms(prim, n, node, r, u):
    def load(k):
        return [prim[q, node(k), r, :] for q in range(7)]

    acc = [[None] * 4 for _ in range(5)]
    for i in range(5):
        for j in range(i + 1, 5):
            q = float(2.0 * WEIGHTS[i] * DERIV[i, j])
            flux = pair_flux(load(i), load(j), n, q)
            for v in range(4):
                term = flux[v]
                acc[i][v] = term if acc[i][v] is None else acc[i][v] + term
                acc[j][v] = -term if acc[j][v] is None else acc[j][v] - term
    hn = HX if n == 0 else HY

    def half(k):
        c = [u[v, node(k), r, :] for v in range(4)]
        speed = prim[hn, node(k), r, :]
        p = prim[PR, node(k), r, :]
        h = [0.5 * c[1 + n], speed * c[1], speed * c[2], speed * (0.5 * c[3] + p)]
        h[1 + n] = h[1 + n] + p
        return c, h, jnp.abs(speed) + prim[HC, node(k), r, :]

    before = half(0)
    prev = None
    outs = []
    for k in range(5):
        if k < 4:
            after = half(k + 1)
            fast = jnp.maximum(before[2], after[2])
            g = [
                before[1][v] + after[1][v]
                - (fast if v < 3 else 0.5 * fast) * (after[0][v] - before[0][v])
                for v in range(4)
            ]
            before = after
        for v in range(4):
            if k == 0:
                t = g[v]
            elif k == 4:
                t = -prev[v]
            else:
                t = g[v] - prev[v]
            w = WINV[k] * ENERGY[v]
            outs.append((k, v, acc[k][v] * -w, (acc[k][v] - t) * w))
        prev = g
    return outs


def finished_column(i, rx, sx, fy, blend, sink):
    def inner(h, c):
        r = tile(h)
        share = blend[r, :]
        for k in range(5):
            m = k * 5 + i
            for v in range(4):
                rate = rx[v, m, r, :] + share * sx[v, m, r, :]
                if k == 0:
                    rate = rate + WINV[0] * fy[i, 0, v, r, :]
                if k == 4:
                    rate = rate - WINV[4] * fy[i, 1, v, r, :]
                sink(v, k, m, r, rate)
        return c

    lax.fori_loop(0, blend.shape[0] // 8, inner, 0)


def column_y(i, prim, rx, sx, fy, blend, u, sink):
    def inner(h, c):
        r = tile(h)
        share = blend[r, :]
        for k, v, vol, diff in line_terms(prim, 1, lambda k: k * 5 + i, r, u):
            m = k * 5 + i
            rate = (rx[v, m, r, :] + vol) + share * (sx[v, m, r, :] + diff)
            if k == 0:
                rate = rate + WINV[0] * fy[i, 0, v, r, :]
            if k == 4:
                rate = rate - WINV[4] * fy[i, 1, v, r, :]
            sink(v, k, m, r, rate)
        return c

    lax.fori_loop(0, blend.shape[0] // 8, inner, 0)


def volume_y(prim, rx, sx, fy, blend, u, out):
    def body(early, i, carry):
        def sink(v, k, m, r, rate):
            out[v, m, r, :] = rate

        if early:
            finished_column(i, rx, sx, fy, blend, sink)
        else:
            column_y(i, prim, rx, sx, fy, blend, u, sink)
        return carry

    lax.fori_loop(0, EARLY, functools.partial(body, True), 0)
    lax.fori_loop(EARLY, 5, functools.partial(body, False), 0)


def kernel(
    ngx, ngy, state_hbm, state, prim, first, rx, sx, fy, blend, step_ref,
    rate, product, fx, raw, packx, packy, gotx, goty,
    edge, top, top_got,
    ins, hs, hr, ts, tr,
):
    loads = [
        pltpu.make_async_copy(
            state_hbm.at[:, pl.ds(a * 5, 5)], state.at[:, pl.ds(a * 5, 5)], ins.at[a]
        )
        for a in range(5)
    ]
    for copy in loads:
        copy.start()
    gx = lax.axis_index("gx")
    gy = lax.axis_index("gy")
    at_x = lambda d: (lax.rem(gx + d, ngx), gy)
    at_y = lambda d: (gx, lax.rem(gy + d, ngy))
    rows = state.shape[2]
    halves = rows // 8

    barrier = pltpu.get_barrier_semaphore()
    peers = [
        (lax.rem(gx + d // ngy, ngx), lax.rem(gy + d % ngy, ngy)) for d in range(1, ngx * ngy)
    ]
    for peer in peers:
        pl.semaphore_signal(barrier, inc=1, device_id=peer, device_id_type=MESH)

    lane = lax.broadcasted_iota(jnp.int32, (rows, LANES), 1)
    row = lax.broadcasted_iota(jnp.int32, (rows, LANES), 0)

    def remote(src, dst, send, recv, device):
        return pltpu.make_async_remote_copy(
            src_ref=src, dst_ref=dst, send_sem=send, recv_sem=recv,
            device_id=device, device_id_type=MESH,
        )

    def halo_copies(sec):
        return [
            remote(packx.at[sec, 0], gotx.at[sec, 0], hs.at[sec, 0], hr.at[sec, 0], at_x(1)),
            remote(packx.at[sec, 1], gotx.at[sec, 1], hs.at[sec, 1], hr.at[sec, 1], at_x(ngx - 1)),
            remote(packy.at[sec, 0], goty.at[sec, 0], hs.at[sec, 2], hr.at[sec, 2], at_y(1)),
            remote(packy.at[sec, 1], goty.at[sec, 1], hs.at[sec, 3], hr.at[sec, 3], at_y(ngy - 1)),
        ]

    def indicator(sec):
        def body(h, carry):
            r = tile(h)
            lines = []
            for a in range(5):
                lines.append(
                    transform(
                        [product[a * 5 + b, r, :] for b in range(5)]
                    )
                )
            sums = {}
            for l in range(5):
                modes = transform([lines[a][l] for a in range(5)])
                for k in range(5):
                    level = max(k, l)
                    sq = modes[k] * modes[k]
                    key = level if level >= 3 else 0
                    sums[key] = sums[key] + sq if key in sums else sq
            lower = sums[0] + sums[3]
            total = lower + sums[4]
            level = jnp.maximum(sums[4] / total, sums[3] / lower)
            threshold = 0.5 * 10.0 ** (-1.8 * 5.0**0.25)
            sharp = math.log((1.0 - 0.0001) / 0.0001)
            value = 1.0 / (1.0 + jnp.exp((-sharp / threshold) * (level - threshold)))
            raw[r, :] = jnp.minimum(value, 0.5)
            return carry

        lax.fori_loop(0, halves, body, 0)

    def pack(sec, u):
        hi = jnp.where(lane == 5, pltpu.roll(raw[...], 6, 1), 0.0)
        lo = jnp.where(lane == 5, pltpu.roll(raw[...], 5, 1), 0.0)
        for v in range(4):
            for a in range(5):
                k = v * 8 + a
                hi = jnp.where(lane == k, pltpu.roll(u[v, a * 5 + 4], k + 1, 1), hi)
                low = u[v, a * 5]
                lo = jnp.where(lane == k, pltpu.roll(low, k, 1) if k else low, lo)
        packx[sec, 0] = hi
        packx[sec, 1] = lo
        packy[sec] = jnp.zeros(packy.shape[1:], F32)
        for v in range(4):
            for b in range(5):
                k = v * 8 + b
                packy[sec, 0, k : k + 1, :] = u[v, 20 + b, rows - 1 : rows, :]
                packy[sec, 1, k : k + 1, :] = u[v, b, 0:1, :]
        packy[sec, 0, 5:6, :] = raw[rows - 1 : rows, :]
        packy[sec, 1, 5:6, :] = raw[0:1, :]

    def faces(u):
        def body(i, carry):
            hi, lo = i * 5 + 4, i * 5
            l = [pltpu.roll(prim[q, hi], 1, 1) for q in range(8)]
            r = [prim[q, lo] for q in range(8)]
            flux = face_of(l, r, pltpu.roll(u[3, hi], 1, 1), u[3, lo], 0)
            for v in range(4):
                fx[i, 0, v] = flux[v]
                fx[i, 1, v] = pltpu.roll(flux[v], LANES - 1, 1)
            hi, lo = 20 + i, i
            l = [pltpu.roll(prim[q, hi], 1, 0) for q in range(8)]
            r = [prim[q, lo] for q in range(8)]
            flux = face_of(l, r, pltpu.roll(u[3, hi], 1, 0), u[3, lo], 1)
            for v in range(4):
                fy[i, 0, v] = flux[v]
                fy[i, 1, v] = pltpu.roll(flux[v], rows - 1, 0)
            return carry

        lax.fori_loop(0, 5, body, 0)

    def volume_x(u):
        def body(i, carry):
            def inner(h, c):
                r = tile(h)
                for k, v, vol, diff in line_terms(prim, 0, lambda k: i * 5 + k, r, u):
                    rx[v, i * 5 + k, r, :] = vol
                    sx[v, i * 5 + k, r, :] = diff
                return c

            return lax.fori_loop(0, halves, inner, carry)

        lax.fori_loop(0, 5, body, 0)

    def finish_halo(sec):
        hi, lo = packx[sec, 0], packx[sec, 1]
        from_left, from_right = gotx[sec, 0], gotx[sec, 1]
        lslab = jnp.where(lane < 64, from_left, pltpu.roll(hi, 64, 1))
        rslab = jnp.where(lane < 64, lo, pltpu.roll(from_right, 64, 1))
        lu = [lslab if v == 0 else pltpu.roll(lslab, LANES - 8 * v, 1) for v in range(4)]
        ru = [rslab if v == 0 else pltpu.roll(rslab, LANES - 8 * v, 1) for v in range(4)]
        flux = face_of(primitives_of(lu), primitives_of(ru), lu[3], ru[3], 0)
        for a in range(5):
            for v in range(4):
                low = pltpu.roll(flux[v], LANES - a, 1) if a else flux[v]
                high = pltpu.roll(flux[v], 63 - a, 1)
                flo = jnp.where(lane == 0, low, fx[a, 0, v])
                fhi = jnp.where(lane == LANES - 1, high, fx[a, 1, v])
                rx[v, a * 5] = rx[v, a * 5] + WINV[0] * flo
                rx[v, a * 5 + 4] = rx[v, a * 5 + 4] - WINV[4] * fhi
        for side in range(2):
            lsrc = goty.at[sec, 0] if side == 0 else packy.at[sec, 0]
            rsrc = packy.at[sec, 1] if side == 0 else goty.at[sec, 1]
            lu = [lsrc[8 * v : 8 * v + 8, :] for v in range(4)]
            ru = [rsrc[8 * v : 8 * v + 8, :] for v in range(4)]
            flux = face_of(primitives_of(lu), primitives_of(ru), lu[3], ru[3], 1)
            for v in range(4):
                edge[side, v] = flux[v]
        for b in range(5):
            for v in range(4):
                fy[b, 0, v, 0:1, :] = edge[0, v, b : b + 1, :]
                fy[b, 1, v, rows - 1 : rows, :] = edge[1, v, b : b + 1, :]
        own = raw[...]
        left = jnp.where(lane == 0, pltpu.roll(from_left, LANES - 5, 1), pltpu.roll(own, 1, 1))
        right = jnp.where(
            lane == LANES - 1, pltpu.roll(from_right, LANES - 6, 1), pltpu.roll(own, LANES - 1, 1)
        )
        below = jnp.where(row == 0, goty[sec, 0, 5:6, :], pltpu.roll(own, 1, 0))
        above = jnp.where(row == rows - 1, goty[sec, 1, 5:6, :], pltpu.roll(own, rows - 1, 0))
        beside = jnp.maximum(jnp.maximum(left, right), jnp.maximum(below, above))
        blend[...] = jnp.maximum(own, 0.5 * beside)

    def early_column(u, i, carry):
        def inner(h, c):
            r = tile(h)
            for k, v, vol, diff in line_terms(prim, 1, lambda k: k * 5 + i, r, u):
                m = k * 5 + i
                rx[v, m, r, :] = rx[v, m, r, :] + vol
                sx[v, m, r, :] = sx[v, m, r, :] + diff
            return c

        return lax.fori_loop(0, halves, inner, carry)

    def prepare(a, fastest):
        for m in [a * 5 + b for b in range(5)]:
            q = primitives_of([state[v, m] for v in range(4)])
            for f in range(8):
                prim[f, m] = q[f]
            product[m] = q[RHO] * q[PR]
            speed = jnp.sqrt(q[HX] * q[HX] + q[HY] * q[HY]) + q[HC]
            fastest = jnp.maximum(fastest, speed)
        return fastest

    def load_and_prepare(a, fastest):
        pltpu.make_async_copy(
            state_hbm.at[:, pl.ds(a * 5, 5)], state.at[:, pl.ds(a * 5, 5)], ins.at[a]
        ).wait()
        return prepare(a, fastest)

    fastest = lax.fori_loop(0, 5, load_and_prepare, jnp.zeros((rows, LANES), F32))
    local_top = fastest[0:8]
    for h in range(1, halves):
        local_top = jnp.maximum(local_top, fastest[8 * h : 8 * h + 8])
    top[...] = jnp.broadcast_to(jnp.max(local_top, axis=0, keepdims=True), (8, LANES))
    indicator(0)
    pack(0, state)
    pl.semaphore_wait(barrier, ngx * ngy - 1)
    halos = halo_copies(0)
    for copy in halos:
        copy.start()
    for d, peer in enumerate(peers):
        remote(
            top.at[pl.ds(0, 1)], top_got.at[d, pl.ds(0, 1)], ts.at[0], tr.at[0], peer
        ).start()
    faces(state)
    volume_x(state)
    lax.fori_loop(0, EARLY, functools.partial(early_column, state), 0)
    for copy in halos:
        copy.wait()
    finish_halo(0)
    volume_y(prim, rx, sx, fy, blend, state, rate)
    every = top_got.at[:, pl.ds(0, 1)]
    tops = remote(every, every, ts.at[0], tr.at[0], peers[0])
    tops.wait_recv()
    best = top[0:1, :]
    for d in range(len(peers)):
        best = jnp.maximum(best, top_got[d, 0:1, :])
    step = (COURANT * 2.0 / 9.0) / (2.0 * jnp.max(best, axis=1, keepdims=True))
    step = jnp.broadcast_to(step, (8, LANES))
    step_full = jnp.concatenate([step] * halves, axis=0)

    def advance(a, carry):
        for m in [a * 5 + b for b in range(5)]:
            u = [state[v, m] + step_full * rate[v, m] for v in range(4)]
            for v in range(4):
                first[v, m] = u[v]
            product[m] = u[0] * u[3] - 0.5 * (u[1] * u[1] + u[2] * u[2])
        return carry

    lax.fori_loop(0, 5, advance, 0)
    indicator(1)
    pack(1, first)
    halos = halo_copies(1)
    for copy in halos:
        copy.start()
    step_ref[...] = step

    def prepare2(a, carry):
        for m in [a * 5 + b for b in range(5)]:
            q = primitives_of([first[v, m] for v in range(4)])
            for f in range(8):
                prim[f, m] = q[f]
        return carry

    lax.fori_loop(0, 5, prepare2, 0)
    faces(first)
    volume_x(first)
    lax.fori_loop(0, EARLY, functools.partial(early_column, first), 0)
    tops.wait_send()
    for copy in halos:
        copy.wait()
    finish_halo(1)


def last_kernel(state, prim, first, rx, sx, fy, blend, step_ref, adv, tend, adv_v, tend_v, sems):
    step = step_ref[...]

    def column(i):
        pairs = ((adv_v, adv), (tend_v, tend))
        return [
            pltpu.make_async_copy(src.at[i], dst.at[:, :, i], sems.at[k, i])
            for k, (src, dst) in enumerate(pairs)
        ]

    def body(early, i, carry):
        def sink(v, k, m, r, rate):
            tend_v[i, v, k, r, :] = rate
            adv_v[i, v, k, r, :] = 0.5 * state[v, m, r, :] + 0.5 * (
                first[v, m, r, :] + step * rate
            )

        if early:
            finished_column(i, rx, sx, fy, blend, sink)
        else:
            column_y(i, prim, rx, sx, fy, blend, first, sink)
        for copy in column(i):
            copy.start()
        return carry

    lax.fori_loop(0, EARLY, functools.partial(body, True), 0)
    lax.fori_loop(EARLY, 5, functools.partial(body, False), 0)
    for i in range(5):
        for copy in column(i):
            copy.wait()


def local(ngx, ngy, state):
    shape = state.shape
    rows, cols = shape[3], shape[4]
    flat = (4, 25, rows, cols)
    vmem = lambda *s: pltpu.VMEM(s, F32)
    whole = pl.BlockSpec(memory_space=pltpu.VMEM)
    hbm = pl.BlockSpec(memory_space=pltpu.HBM)
    mid = [flat, (8, 25, rows, cols), flat, flat, flat, (5, 2, 4, rows, cols), (rows, cols), (8, cols)]
    kept = pl.pallas_call(
        functools.partial(kernel, ngx, ngy),
        out_shape=[jax.ShapeDtypeStruct(m, F32) for m in mid],
        in_specs=[hbm],
        out_specs=[whole] * len(mid),
        scratch_shapes=[
            vmem(*flat), vmem(25, rows, cols), vmem(5, 2, 4, rows, cols), vmem(rows, cols),
            vmem(2, 2, rows, cols), vmem(2, 2, 32, cols),
            vmem(2, 2, rows, cols), vmem(2, 2, 32, cols),
            vmem(2, 4, 8, cols),
            vmem(8, cols), vmem(ngx * ngy - 1, 8, cols),
            pltpu.SemaphoreType.DMA((5,)),
            pltpu.SemaphoreType.DMA((2, 4)), pltpu.SemaphoreType.DMA((2, 4)),
            pltpu.SemaphoreType.DMA((1,)), pltpu.SemaphoreType.DMA((1,)),
        ],
        compiler_params=pltpu.CompilerParams(collective_id=0, has_side_effects=True,
                                             vmem_limit_bytes=16 * 1024 * 1024),
        name="dg_sections",
    )(pltpu.with_memory_space_constraint(state.reshape(flat), pltpu.HBM))
    return pl.pallas_call(
        last_kernel,
        out_shape=(jax.ShapeDtypeStruct(shape, F32),) * 2,
        in_specs=[whole] * len(mid),
        out_specs=[hbm] * 2,
        scratch_shapes=[
            vmem(5, 4, 5, rows, cols), vmem(5, 4, 5, rows, cols), pltpu.SemaphoreType.DMA((2, 5))
        ],
        compiler_params=pltpu.CompilerParams(vmem_limit_bytes=16 * 1024 * 1024),
        name="dg_last_pass",
    )(*kept)


def solution(mesh):
    spec = P(None, None, None, "gy", "gx")
    return jax.shard_map(
        functools.partial(local, mesh.shape["gx"], mesh.shape["gy"]),
        mesh=mesh,
        in_specs=(spec,),
        out_specs=(spec, spec),
        check_vma=False,
    )
```
